512 devices in a mesh: rows: 128 (over z, x, core), cols: 4 (over y).
Axes of the slice: x: 4, y: 4, z: 16, core: 2. Of those that a mesh axis runs over, the one named last changes fastest.
Arguments:
- tile_density: bfloat16 [32768, 64, 64], P(('rows', 'cols')), may hold values from -6 to 6
- tile_dest: int32 [32768, 1], P(('rows', 'cols')), may hold values from 0 to 127; in each aligned block of 64 rows (0 to 63, 64 to 127, ...) at most 2 rows name the same one
- tile_place: int32 [32768], P(('rows', 'cols')), may hold values from 0 to 31
- psf_spectrum: bfloat16 [32768, 2048], P('rows', 'cols'), may hold values from 0.049804688 to 1
Outputs:
- flare_spectrum: float32 [32768, 2, 2048], P('rows', None, 'cols')
The draws below stay inside these ranges and needn't reach their ends.
Inputs may be any that keep to these rules, and one draw needn't show every extreme that they name: `tile_dest`: among the 64 tiles of one owner, at most 2 lie in the same row slab, and some owner has exactly 2 in one row slab.
All inputs are finite; a program needn't handle non-finite values.
Results may differ from the reference program's by a relative error of at most 0.0075.
Values may be sent and summed in bfloat16 or wider, within the bound.
No kernel may reach another device: no remote copies, remote signals or barrier semaphores. Data moves between devices by JAX's collectives and lax.ppermute only.
A program may use at most 64 MiB of HBM per device.

```python
import math
import jax
import jax.numpy as jnp
import numpy as np
from jax import lax

ROWS_DEV = 256
COLS_DEV = 512
TILE = 64
OWNER_TILES = 64
GRID_ROWS = 32768
SLAB_COLS = 2048
CAPACITY = 2
ALL_TILES = 32768
N_ROWS = 128
N_COLS = 4


def place_ends(values, stream_key, smallest, largest):
    longest = values.shape.index(max(values.shape))
    spots = []
    for shift in (0, 1):
        where = [jax.random.randint(jax.random.fold_in(stream_key, axis), (), 0, length) for axis, length in enumerate(values.shape)]
        where[longest] = (where[longest] + shift) % values.shape[longest]
        spots.append(tuple(where))
    return values.at[spots[0]].set(smallest).at[spots[1]].set(largest)


def levels(stream_key, dims, shards, low, largest):
    def one(axis_at, parts):
        heights = jax.random.uniform(jax.random.fold_in(jax.random.fold_in(stream_key, 6), axis_at), (parts,), jnp.float32, low / len(shards), largest / len(shards))
        return jnp.repeat(jnp.exp(heights), dims[axis_at] // parts).reshape((-1,) + (1,) * (len(dims) - axis_at - 1))

    level = one(*shards[0])
    for cut in shards[1:]:
        level = level * one(*cut)
    return level


def shared_out(stream_key, own, number, rows, number_of, top, bound, lean):
    sequence = jax.random.permutation(stream_key, number_of)
    heavy_load, ordinary = shares(number_of, rows * top, bound, lean, True), shares(number_of, rows * top, bound, lean, False)
    places = jnp.arange(number_of)

    def named(sizes, rotation):
        used = int((sizes > 0).sum())
        fixed = max(1, used // 4)
        passed = fixed + (places - fixed + rotation * (used - fixed)) % max(1, number_of - fixed)
        return jnp.zeros((number_of,), jnp.int32).at[sequence[jnp.where(places < fixed, places, passed)]].set(jnp.asarray(sizes, jnp.int32))

    sizes = jnp.where(number % 4 == 0, named(heavy_load, number // 4), named(ordinary, number - number // 4 - 1))
    mixed = jax.random.permutation(jax.random.fold_in(own, 3), number_of)
    source_of, receiver = mixed[0:number_of // 2 * 2:2], mixed[1:number_of // 2 * 2:2]
    slack = jnp.minimum(sizes[source_of] - 1, bound - sizes[receiver]) // 2
    slack = jnp.where((source_of == sequence[0]) | (receiver == sequence[0]) | (sizes[receiver] == 0), 0, jnp.maximum(slack, 0))
    passed = jax.random.randint(jax.random.fold_in(own, 4), (number_of // 2,), 0, 1 << 20) % (slack + 1)
    sizes = sizes.at[source_of].add(-passed).at[receiver].add(passed)
    labels = jnp.searchsorted(jnp.cumsum(sizes), jnp.arange(rows * top), side="right").astype(jnp.int32)
    grid = labels.reshape(top, rows).T
    grid = grid[jax.random.permutation(jax.random.fold_in(own, 1), rows)]
    rotation = jax.random.randint(jax.random.fold_in(own, 2), (rows, 1), 0, top)
    return jnp.take_along_axis(grid, (jnp.arange(top)[None, :] + rotation) % top, axis=1)


def shares(amount, total, bound, skew, full):
    portions = [(1 << 20) // math.isqrt(grade ** skew) + 1 for grade in range(1, amount + 1)]
    largest = bound if full else min(bound, max(-(-total // amount), total * portions[0] // sum(portions)))
    least = 1 if total - largest >= amount - 1 else 0
    counts, spare = [largest] + [least] * (amount - 1), total - largest - least * (amount - 1)
    while spare > 0:
        candidates = [i for i in range(1, amount) if counts[i] < largest] or [i for i in range(1, amount) if counts[i] < bound]
        whole, left = sum([portions[i] for i in candidates]), spare
        for i in candidates:
            more = min(bound - counts[i], max(1, left * portions[i] // whole), spare)
            counts[i] = counts[i] + more
            spare = spare - more
    return np.array(counts)


def scatter_about(own_key, extent, width, bound, split=(), kind=jnp.bfloat16):
    level = levels(own_key, extent, split, -0.22, 0.18) if split else 1.0
    array = jax.random.normal(own_key, extent, jnp.float32) * width * level
    return jnp.minimum(jnp.maximum(array, -bound), bound).astype(kind)


def setup_inputs(seed: int = 0) -> dict:
    arg_keys = jax.random.split(jax.random.key(seed), 5)
    tile_density = scatter_about(arg_keys[0], (ALL_TILES, TILE, TILE), 1.0, 6.0, ((0, 512),))
    tile_dest_keys = jax.random.split(jax.random.fold_in(arg_keys[1], 1), ALL_TILES // OWNER_TILES)
    tile_dest_turns = jax.random.permutation(jax.random.fold_in(arg_keys[1], 3), ALL_TILES // OWNER_TILES)
    tile_dest = jax.vmap(lambda own, number: shared_out(jax.random.fold_in(arg_keys[1], 2), own, number, OWNER_TILES, N_ROWS, 1, CAPACITY, 2))(tile_dest_keys, tile_dest_turns).reshape((ALL_TILES, 1))
    tile_place = place_ends(jax.random.randint(arg_keys[2], (ALL_TILES,), 0, (ROWS_DEV // TILE) * (COLS_DEV // TILE)), jax.random.fold_in(arg_keys[2], 1), 0, ((ROWS_DEV // TILE) * (COLS_DEV // TILE)) - 1).astype(jnp.int32)
    psf_spectrum = jnp.clip(jnp.exp(math.log(1.0) - 2.9996462 * jax.random.uniform(arg_keys[3], (GRID_ROWS, SLAB_COLS), jnp.float32) ** levels(arg_keys[3], (GRID_ROWS, SLAB_COLS), ((0, 128), (1, 4)), -0.2, 0.2)), 0.049804688, 1.0).astype(jnp.bfloat16)
    return dict(tile_density=tile_density, tile_dest=tile_dest, tile_place=tile_place, psf_spectrum=psf_spectrum)


def make_table(length, factor):
    positions = jnp.arange(length, dtype=jnp.int32)
    angles = 2.0 * math.pi / length * (positions[:, None] * positions[None, :] % length).astype(jnp.float32)
    cosine = jnp.cos(angles) * factor
    sine_part = jnp.sin(angles) * factor
    upper_rows = jnp.stack([cosine, -sine_part], 1)
    bottom = jnp.stack([sine_part, cosine], 1)
    return jnp.stack([upper_rows, bottom], 0).astype(jnp.bfloat16)

def twiddle(real_part, imag_part, position, frequency, period):
    angles = 2.0 * math.pi / period * (position * frequency % period).astype(jnp.float32)
    cosine = jnp.cos(angles)
    sine_part = jnp.sin(angles)
    return (real_part * cosine + imag_part * sine_part, imag_part * cosine - real_part * sine_part)

def reference(tile_density, tile_dest, tile_place, psf_spectrum):
    per_row = COLS_DEV // TILE
    tile_index = jnp.arange(ALL_TILES, dtype=jnp.int32)
    owner_col = tile_index // OWNER_TILES % N_COLS
    tile_row = ROWS_DEV // TILE * tile_dest[:, 0] + tile_place // per_row
    tile_col = per_row * owner_col + tile_place % per_row
    grid_cols = SLAB_COLS // TILE
    flat_index = (tile_row * grid_cols + tile_col).astype(jnp.int32)
    tile_sums = jnp.zeros((GRID_ROWS // TILE * grid_cols, TILE, TILE), jnp.float32)
    tile_sums = tile_sums.at[flat_index].add(tile_density.astype(jnp.float32))
    density_grid = tile_sums.reshape(GRID_ROWS // TILE, grid_cols, TILE, TILE).transpose(0, 2, 1, 3)
    density_grid = lax.optimization_barrier(density_grid.reshape(GRID_ROWS, SLAB_COLS).astype(jnp.bfloat16))
    blocks = density_grid.reshape(GRID_ROWS, N_COLS, COLS_DEV).astype(jnp.float32)
    row_table = make_table(COLS_DEV, 1.0 / math.sqrt(SLAB_COLS)).reshape(2 * COLS_DEV, 2 * COLS_DEV).astype(jnp.float32)
    col_table = make_table(N_ROWS, 1.0).transpose(3, 2, 1, 0).astype(jnp.float32)
    final_table = make_table(ROWS_DEV, 1.0 / math.sqrt(GRID_ROWS)).transpose(3, 2, 1, 0)
    final_table = final_table.reshape(2 * ROWS_DEV, 2 * ROWS_DEV).astype(jnp.float32)
    owners = jnp.arange(N_COLS, dtype=jnp.int32)
    columns = jnp.arange(COLS_DEV, dtype=jnp.int32)
    row_index = jnp.arange(ROWS_DEV, dtype=jnp.int32)
    row_freq = jnp.arange(N_ROWS, dtype=jnp.int32)
    highest = lax.Precision.HIGHEST

    def one_block(frequency):
        angles = 2.0 * math.pi / N_COLS * (owners * frequency % N_COLS).astype(jnp.float32)
        sum_real = jnp.einsum('jef,e->jf', blocks, jnp.cos(angles), precision=highest)
        sum_imag = -jnp.einsum('jef,e->jf', blocks, jnp.sin(angles), precision=highest)
        real_part, imag_part = twiddle(sum_real, sum_imag, columns[None, :], frequency, SLAB_COLS)
        section_one = lax.optimization_barrier(jnp.concatenate([real_part, imag_part], 1).astype(jnp.bfloat16))
        rows_spectrum = jnp.dot(section_one.astype(jnp.float32), row_table, precision=highest)
        rows_spectrum = lax.optimization_barrier(rows_spectrum.astype(jnp.bfloat16))
        values = rows_spectrum.reshape(N_ROWS, ROWS_DEV, 2, COLS_DEV).astype(jnp.float32)
        combined = jnp.einsum('kqap,abpc->kbqc', col_table, values, precision=highest)
        real_two, imag_two = twiddle(combined[:, :, 0], combined[:, :, 1], row_index[None, :, None], row_freq[:, None, None], GRID_ROWS)
        section_two = lax.optimization_barrier(jnp.stack([real_two, imag_two], 2).astype(jnp.bfloat16))
        section_two = section_two.astype(jnp.float32).reshape(N_ROWS, 2 * ROWS_DEV, COLS_DEV)
        result_spec = jnp.einsum('mn,knc->kmc', final_table, section_two, precision=highest)
        result_spec = result_spec.reshape(GRID_ROWS, 2, COLS_DEV)
        psf_block = lax.dynamic_slice_in_dim(psf_spectrum, (frequency * COLS_DEV).astype(jnp.int32), COLS_DEV, 1)
        return result_spec * psf_block.astype(jnp.float32)[:, None, :]
    spectra = lax.map(one_block, jnp.arange(N_COLS, dtype=jnp.int32))
    return spectra.transpose(1, 2, 0, 3).reshape(GRID_ROWS, 2, SLAB_COLS)
```

```python
import math

import jax
import jax.numpy as jnp
from jax import lax
from jax.experimental import pallas as pl
from jax.experimental.pallas import tpu as pltpu
from jax.sharding import Mesh
from jax.sharding import PartitionSpec as P

ROWS = ("chip", "core")
GROUP = ("core", "cols")
F32 = jnp.float32
BF16 = jnp.bfloat16


def table_parts(inputs, outputs, length, factor):
    angles = 2.0 * math.pi / length * (inputs * outputs % length).astype(F32)
    return jnp.cos(angles) * factor, jnp.sin(angles) * factor


def twiddle_parts(position, frequency, period):
    angles = 2.0 * math.pi / period * (position * frequency % period).astype(F32)
    return jnp.cos(angles), jnp.sin(angles)


def lane_group(shape):
    return lax.broadcasted_iota(jnp.int32, shape, 1) // 32


def pack_body(tiles_ref, out_ref):
    group = lane_group((16, 128))
    for block in range(tiles_ref.shape[1] // 128):
        parts = [
            tiles_ref[16 * g : 16 * g + 16, 128 * block : 128 * block + 128].astype(F32)
            for g in range(4)
        ]
        for quarter in range(4):
            value = None
            for g in range(4):
                shift = 32 * ((g - quarter) % 4)
                moved = pltpu.roll(parts[g], shift, 1) if shift else parts[g]
                value = moved if value is None else jnp.where(group == g, moved, value)
            out_ref[4 * block + quarter] = value.astype(BF16)


def scatter_body(slab_hot_ref, place_ref, tiles_ref, out_ref, spread_ref, sum_ref):
    step = pl.program_id(0)
    rows = tiles_ref.shape[0]
    values = tiles_ref[...].astype(F32)
    group = lane_group(values.shape)
    rolls = [values] + [pltpu.roll(values, 32 * j, 1) for j in range(1, 4)]
    total = None
    for g in range(4):
        copies = rolls[(-g) % 4]
        for h in range(1, 4):
            copies = jnp.where(group == h, rolls[(h - g) % 4], copies)
        copies = copies.astype(BF16)
        place = place_ref[:, 128 * g : 128 * g + 128]
        for m in range(8):
            spread_ref[g, :, 128 * m : 128 * m + 128] = jnp.where(
                place == jnp.array(4.0 * m, BF16), copies, jnp.zeros_like(copies)
            )
        part = jnp.dot(slab_hot_ref[g], spread_ref[g], preferred_element_type=F32)
        total = part if total is None else total + part

    @pl.when(step == 0)
    def _():
        sum_ref[...] = total

    @pl.when(step > 0)
    def _():
        sum_ref[...] += total

    @pl.when(step == pl.num_programs(0) - 1)
    def _():
        out_ref[...] = sum_ref[...].astype(BF16)


def rows_body(mix_ref, cells_ref, turn_ref, row_table_ref, slab_table_ref, phase_ref, out_ref):
    halves = []
    for low in range(2):
        real, imag = [], []
        for core in range(2):
            parts = [
                cells_ref[4 * core + e, :, 256 * low : 256 * low + 256].astype(F32)
                for e in range(4)
            ]
            sum_real = parts[0] * mix_ref[0]
            sum_imag = -(parts[0] * mix_ref[4])
            for e in range(1, 4):
                sum_real = sum_real + parts[e] * mix_ref[e]
                sum_imag = sum_imag - parts[e] * mix_ref[4 + e]
            cosine = turn_ref[0:1, 256 * core : 256 * core + 256]
            sine = turn_ref[1:2, 256 * core : 256 * core + 256]
            real.append(sum_real * cosine + sum_imag * sine)
            imag.append(sum_imag * cosine - sum_real * sine)
        halves.append(jnp.concatenate(real + imag, 1).astype(BF16))
    spectrum = jnp.dot(
        jnp.concatenate(halves, 0), row_table_ref[...], preferred_element_type=F32
    ).astype(BF16)
    for low in range(2):
        half = spectrum[128 * low : 128 * low + 128]
        stacked = jnp.concatenate([half[:, :512], half[:, 512:]], 0)
        combined = jnp.dot(slab_table_ref[...], stacked, preferred_element_type=F32)
        cosine = phase_ref[:, 2 * low : 2 * low + 1]
        sine = phase_ref[:, 2 * low + 1 : 2 * low + 2]
        real, imag = combined[:128], combined[128:]
        out_ref[2 * low] = (real * cosine + imag * sine).astype(BF16)
        out_ref[2 * low + 1] = (imag * cosine - real * sine).astype(BF16)


def whole(shape, space=pltpu.VMEM):
    return pl.BlockSpec(shape, lambda *_: (0,) * len(shape), memory_space=space)


def on_device(tile_density, tile_dest, tile_place, psf_spectrum):
    chip = lax.axis_index("chip")
    core = lax.axis_index("core")
    me_col = lax.axis_index("cols")
    iota = lambda n: jnp.arange(n, dtype=jnp.int32)

    tiles_flat = tile_density.reshape(64, 4096)
    outgoing = pl.pallas_call(
        pack_body, out_shape=jax.ShapeDtypeStruct((128, 16, 128), BF16)
    )(tiles_flat)
    arrived = lax.all_to_all(outgoing, ROWS, 0, 0, tiled=True)
    codes = tile_dest[:, 0] * 32 + tile_place
    labels = lax.all_to_all(jnp.broadcast_to(codes[None], (128, 64)), ROWS, 0, 0, tiled=True)

    slabs = (labels // 32).reshape(128, 4, 16).transpose(1, 0, 2).reshape(4, 1, 2048)
    slab_hot = (slabs == iota(128)[None, :, None]).astype(BF16)
    places = (labels % 32).reshape(128, 4, 16).transpose(0, 2, 1).reshape(2048, 4, 1)
    places = (places - (iota(128) // 32)[None, None, :]).astype(BF16).reshape(2048, 512)

    step_rows = 256
    grid_cells = pl.pallas_call(
        scatter_body,
        grid=(2048 // step_rows,),
        in_specs=[
            pl.BlockSpec((4, 128, step_rows), lambda i: (0, 0, i)),
            pl.BlockSpec((step_rows, 512), lambda i: (i, 0)),
            pl.BlockSpec((step_rows, 128), lambda i: (i, 0)),
        ],
        out_specs=pl.BlockSpec((128, 1024), lambda i: (0, 0)),
        out_shape=jax.ShapeDtypeStruct((128, 1024), BF16),
        scratch_shapes=[
            pltpu.VMEM((4, step_rows, 1024), BF16),
            pltpu.VMEM((128, 1024), F32),
        ],
    )(slab_hot, places, arrived.reshape(2048, 128))

    halves = jnp.stack([grid_cells[:, :512], grid_cells[:, 512:]], 0)
    sent = jnp.broadcast_to(halves[:, None], (2, 4, 128, 512)).reshape(8, 128, 512)
    cells = lax.all_to_all(sent, GROUP, 0, 0, tiled=True)

    order = iota(512)
    column = order % 256 // 32 * 64 + order // 256 * 32 + order % 32
    cosine, sine = table_parts(
        column[:, None], iota(512)[None, :], 512, 1.0 / math.sqrt(2048)
    )
    row_table = jnp.concatenate(
        [jnp.concatenate([cosine, -sine], 1), jnp.concatenate([sine, cosine], 1)], 0
    ).astype(BF16)
    cosine, sine = table_parts(iota(128)[:, None], iota(128)[None, :], 128, 1.0)
    slab_table = jnp.concatenate(
        [jnp.concatenate([cosine, sine], 1), jnp.concatenate([-sine, cosine], 1)], 0
    ).astype(BF16)
    angles = 2.0 * math.pi / 4 * (iota(4) * me_col % 4).astype(F32)
    mix = jnp.concatenate([jnp.cos(angles), jnp.sin(angles)])
    turn = jnp.stack(twiddle_parts(column, me_col, 2048), 0)
    phases = []
    for low in range(2):
        phases += twiddle_parts(64 * (2 * core + low) + chip, iota(128), 32768)
    phase = jnp.stack(phases, 1)

    section_two = pl.pallas_call(
        rows_body,
        in_specs=[
            pl.BlockSpec(memory_space=pltpu.SMEM),
            whole((8, 128, 512)),
            whole((2, 512)),
            whole((1024, 1024)),
            whole((256, 256)),
            whole((128, 4)),
        ],
        out_specs=whole((4, 128, 512)),
        out_shape=jax.ShapeDtypeStruct((4, 128, 512), BF16),
    )(mix, cells, turn, row_table, slab_table, phase)

    section_two = lax.all_to_all(
        section_two.transpose(1, 0, 2), ROWS, split_axis=0, concat_axis=0, tiled=True
    )

    place = iota(256)
    position = 64 * (place % 4) + place // 4
    cosine, sine = table_parts(
        iota(256)[:, None], position[None, :], 256, 1.0 / math.sqrt(32768)
    )
    final_table = jnp.stack(
        [jnp.stack([cosine, sine], 2), jnp.stack([-sine, cosine], 2)], 1
    ).reshape(512, 512).astype(BF16)
    result = jnp.dot(final_table, section_two.reshape(512, 512), preferred_element_type=F32)
    return result.reshape(256, 2, 512) * psf_spectrum.astype(F32)[:, None, :]


def solution(mesh):
    split = Mesh(
        mesh.devices.reshape(mesh.devices.shape[0] // 2, 2, mesh.devices.shape[1]),
        ("chip", "core", "cols"),
    )
    everywhere = ("chip", "core", "cols")
    in_specs = (P(everywhere, None, None), P(everywhere, None), P(everywhere), P(ROWS, "cols"))
    return jax.shard_map(
        on_device,
        mesh=split,
        in_specs=in_specs,
        out_specs=P(ROWS, None, "cols"),
        check_vma=False,
    )
```

```python
import math

import jax
import jax.numpy as jnp
from jax import lax
from jax.experimental import pallas as pl
from jax.experimental.pallas import tpu as pltpu
from jax.sharding import Mesh
from jax.sharding import PartitionSpec as P

ROWS = ("chip", "core")
GROUP = ("core", "cols")
F32 = jnp.float32
BF16 = jnp.bfloat16


def table_parts(inputs, outputs, length, factor):
    angles = 2.0 * math.pi / length * (inputs * outputs % length).astype(F32)
    return jnp.cos(angles) * factor, jnp.sin(angles) * factor


def twiddle_parts(position, frequency, period):
    angles = 2.0 * math.pi / period * (position * frequency % period).astype(F32)
    return jnp.cos(angles), jnp.sin(angles)


def lane_group(shape):
    return lax.broadcasted_iota(jnp.int32, shape, 1) // 32


def pack_body(tiles_ref, dest_ref, place_ref, out_ref, flat_ref, packed_ref):
    for part in range(4):
        flat_ref[1024 * part : 1024 * part + 1024, :64] = (
            tiles_ref[16 * part : 16 * part + 16].reshape(1024, 64).astype(F32)
        )
    place = place_ref[...]
    labels = jnp.concatenate([place // 16 * 128 + dest_ref[...], place % 16], 1)
    labels = jnp.broadcast_to(labels.astype(F32), (2, 128))
    group = lane_group((16, 128))
    for chip in range(64):
        parts = [flat_ref[pl.ds(1024 * g + chip, 16, stride=64), :] for g in range(4)]
        for core in range(2):
            value = None
            for g in range(4):
                shift = 32 * (g - core) % 128
                moved = pltpu.roll(parts[g], shift, 1) if shift else parts[g]
                value = moved if value is None else jnp.where(group == g, moved, value)
            start = 18 * (2 * chip + core)
            packed_ref[start : start + 16] = value
            packed_ref[start + 16 : start + 18] = labels
    out_ref[...] = packed_ref[...].astype(BF16)


def scatter_body(tiles_ref, out_ref, flat_ref, spread_ref, hot_ref):
    flat_ref[...] = tiles_ref[...].astype(F32)
    labels = flat_ref[pl.ds(16, 128, stride=18), :]
    named = jnp.transpose(labels)
    group = lane_group((128, 128))
    lane = group.astype(F32)
    slab = lax.broadcasted_iota(jnp.int32, (256, 128), 0).astype(F32)
    total = None
    for step in range(16):
        slot = step % 2
        values = flat_ref[pl.ds(step, 128, stride=18), :]
        rolls = [values] + [pltpu.roll(values, 32 * j, 1) for j in range(1, 4)]
        for g in range(4):
            copies = rolls[(-g) % 4]
            for h in range(1, 4):
                copies = jnp.where(group == h, rolls[(h - g) % 4], copies)
            copies = copies.astype(BF16)
            tile = 16 * g + step
            place = jnp.broadcast_to(labels[:, 64 + tile : 65 + tile], (128, 128)) - lane
            place = place.astype(BF16)
            for m in range(4):
                spread_ref[slot, 128 * g : 128 * g + 128, 128 * m : 128 * m + 128] = jnp.where(
                    place == jnp.array(4.0 * m, BF16), copies, jnp.zeros_like(copies)
                )
            hot = jnp.broadcast_to(named[tile : tile + 1, :], (256, 128)) == slab
            hot_ref[slot, :, 128 * g : 128 * g + 128] = jnp.where(hot, 1.0, 0.0).astype(BF16)
        part = jnp.dot(hot_ref[slot], spread_ref[slot], preferred_element_type=F32)
        total = part if total is None else total + part
    total = total.astype(BF16)
    for core in range(2):
        for e in range(4):
            out_ref[4 * core + e] = total[128 * core : 128 * core + 128]


def rows_body(
    mix_ref, cells_ref, turn_ref, row_table_ref, slab_table_ref, phase_ref, out_ref, flat_ref
):
    halves = []
    for low in range(2):
        real, imag = [], []
        for core in range(2):
            parts = [
                cells_ref[4 * core + e, :, 256 * low : 256 * low + 256].astype(F32)
                for e in range(4)
            ]
            sum_real = parts[0] * mix_ref[0]
            sum_imag = -(parts[0] * mix_ref[4])
            for e in range(1, 4):
                sum_real = sum_real + parts[e] * mix_ref[e]
                sum_imag = sum_imag - parts[e] * mix_ref[4 + e]
            cosine = turn_ref[0:1, 256 * core : 256 * core + 256]
            sine = turn_ref[1:2, 256 * core : 256 * core + 256]
            real.append(sum_real * cosine + sum_imag * sine)
            imag.append(sum_imag * cosine - sum_real * sine)
        halves.append(jnp.concatenate(real + imag, 1).astype(BF16))
    spectrum = jnp.dot(
        jnp.concatenate(halves, 0), row_table_ref[...], preferred_element_type=F32
    ).astype(BF16)
    for low in range(2):
        half = spectrum[128 * low : 128 * low + 128]
        stacked = jnp.concatenate([half[:, :512], half[:, 512:]], 0)
        combined = jnp.dot(slab_table_ref[...], stacked, preferred_element_type=F32)
        cosine = phase_ref[:, 2 * low : 2 * low + 1]
        sine = phase_ref[:, 2 * low + 1 : 2 * low + 2]
        real, imag = combined[:128], combined[128:]
        turned = [real * cosine + imag * sine, imag * cosine - real * sine]
        for p in range(2):
            for v in range(4):
                flat_ref[pl.ds(4 * (2 * low + p) + v, 128, stride=16), :] = turned[p][
                    :, 128 * v : 128 * v + 128
                ]
    out_ref[...] = flat_ref[...].astype(BF16)


VMEM = pl.BlockSpec(memory_space=pltpu.VMEM)
SMEM = pl.BlockSpec(memory_space=pltpu.SMEM)


def on_device(tile_density, tile_dest, tile_place, psf_spectrum):
    chip = lax.axis_index("chip")
    core = lax.axis_index("core")
    me_col = lax.axis_index("cols")
    iota = lambda n: jnp.arange(n, dtype=jnp.int32)

    outgoing = pl.pallas_call(
        pack_body,
        in_specs=[VMEM] * 3,
        out_specs=VMEM,
        out_shape=jax.ShapeDtypeStruct((2304, 128), BF16),
        scratch_shapes=[pltpu.VMEM((4096, 128), F32), pltpu.VMEM((2304, 128), F32)],
    )(tile_density, tile_dest.reshape(1, 64), tile_place.reshape(1, 64))
    arrived = lax.all_to_all(outgoing.reshape(128, 9, 2, 128), ROWS, 0, 0, tiled=True)
    sent = pl.pallas_call(
        scatter_body,
        in_specs=[VMEM],
        out_specs=VMEM,
        out_shape=jax.ShapeDtypeStruct((8, 128, 512), BF16),
        scratch_shapes=[
            pltpu.VMEM((2304, 128), F32),
            pltpu.VMEM((2, 512, 512), BF16),
            pltpu.VMEM((2, 256, 512), BF16),
        ],
    )(pltpu.with_memory_space_constraint(arrived.reshape(2304, 128), pltpu.VMEM))

    cells = lax.all_to_all(sent, GROUP, 0, 0, tiled=True)
    cells = pltpu.with_memory_space_constraint(cells, pltpu.VMEM)

    order = iota(512)
    column = order % 256 // 32 * 64 + order // 256 * 32 + order % 32
    cosine, sine = table_parts(
        column[:, None], iota(512)[None, :], 512, 1.0 / math.sqrt(2048)
    )
    row_table = jnp.concatenate(
        [jnp.concatenate([cosine, -sine], 1), jnp.concatenate([sine, cosine], 1)], 0
    ).astype(BF16)
    cosine, sine = table_parts(iota(128)[:, None], iota(128)[None, :], 128, 1.0)
    slab_table = jnp.concatenate(
        [jnp.concatenate([cosine, sine], 1), jnp.concatenate([-sine, cosine], 1)], 0
    ).astype(BF16)
    angles = 2.0 * math.pi / 4 * (iota(4) * me_col % 4).astype(F32)
    mix = jnp.concatenate([jnp.cos(angles), jnp.sin(angles)])
    turn = jnp.stack(twiddle_parts(column, me_col, 2048), 0)
    phases = []
    for low in range(2):
        phases += twiddle_parts(64 * (2 * core + low) + chip, iota(128), 32768)
    phase = jnp.stack(phases, 1)

    section_two = pl.pallas_call(
        rows_body,
        in_specs=[SMEM] + [VMEM] * 5,
        out_specs=VMEM,
        out_shape=jax.ShapeDtypeStruct((2048, 128), BF16),
        scratch_shapes=[pltpu.VMEM((2048, 128), F32)],
    )(
        mix,
        cells,
        turn,
        pltpu.with_memory_space_constraint(row_table, pltpu.VMEM),
        pltpu.with_memory_space_constraint(slab_table, pltpu.VMEM),
        phase,
    )
    section_two = lax.all_to_all(section_two.reshape(128, 16, 128), ROWS, 0, 0, tiled=True)

    place = iota(256)
    position = 64 * (place % 4) + place // 4
    cosine, sine = table_parts(
        iota(256)[:, None], position[None, :], 256, 1.0 / math.sqrt(32768)
    )
    final_table = jnp.stack(
        [jnp.stack([cosine, sine], 2), jnp.stack([-sine, cosine], 2)], 1
    ).reshape(512, 512).astype(BF16)
    section_two = section_two.reshape(512, 512)
    result = jnp.dot(final_table, section_two, preferred_element_type=F32)
    return result.reshape(256, 2, 512) * psf_spectrum.astype(F32)[:, None, :]


def solution(mesh):
    split = Mesh(
        mesh.devices.reshape(mesh.devices.shape[0] // 2, 2, mesh.devices.shape[1]),
        ("chip", "core", "cols"),
    )
    everywhere = ("chip", "core", "cols")
    in_specs = (P(everywhere, None, None), P(everywhere, None), P(everywhere), P(ROWS, "cols"))
    return jax.shard_map(
        on_device,
        mesh=split,
        in_specs=in_specs,
        out_specs=P(ROWS, None, "cols"),
        check_vma=False,
    )
```

```python
import math

import jax
import jax.numpy as jnp
from jax import lax
from jax.experimental import pallas as pl
from jax.experimental.pallas import tpu as pltpu
from jax.sharding import Mesh
from jax.sharding import PartitionSpec as P

ROWS = ("chip", "core")
GROUP = ("core", "cols")
F32 = jnp.float32
BF16 = jnp.bfloat16


def table_parts(inputs, outputs, length, factor):
    angles = 2.0 * math.pi / length * (inputs * outputs % length).astype(F32)
    return jnp.cos(angles) * factor, jnp.sin(angles) * factor


def twiddle_parts(position, frequency, period):
    angles = 2.0 * math.pi / period * (position * frequency % period).astype(F32)
    return jnp.cos(angles), jnp.sin(angles)


def lane_group(shape):
    return lax.broadcasted_iota(jnp.int32, shape, 1) // 32


def pack_body(tiles_ref, dest_ref, place_ref, out_ref, flat_ref, packed_ref):
    for tile in range(32):
        start = 64 * tile
        flat_ref[start : start + 64, :64] = tiles_ref[tile].astype(F32)
        flat_ref[start : start + 64, 64:] = tiles_ref[tile + 32].astype(F32)
    place = place_ref[...]
    labels = jnp.concatenate([place // 16 * 128 + dest_ref[...], place % 16], 1).astype(F32)
    group = lax.broadcasted_iota(jnp.int32, (1, 128), 1) // 16
    swapped = jnp.where(
        group % 2 == 0, pltpu.roll(labels, 112, 1), pltpu.roll(labels, 16, 1)
    )
    labels = [jnp.broadcast_to(row, (2, 128)) for row in (labels, swapped)]
    odd = lane_group((16, 128)) % 2 == 1
    for chip in range(64):
        first = flat_ref[pl.ds(chip, 16, stride=64), :]
        second = flat_ref[pl.ds(1024 + chip, 16, stride=64), :]
        values = [
            jnp.where(odd, pltpu.roll(second, 32, 1), first),
            jnp.where(odd, first, pltpu.roll(second, 96, 1)),
        ]
        for core in range(2):
            start = 18 * (2 * chip + core)
            packed_ref[start : start + 16] = values[core]
            packed_ref[start + 16 : start + 18] = labels[core]
    out_ref[...] = packed_ref[...].astype(BF16)


def scatter_body(tiles_ref, out_ref, flat_ref, spread_ref, hot_ref):
    flat_ref[...] = tiles_ref[...].astype(F32)
    labels = flat_ref[pl.ds(16, 128, stride=18), :]
    named = jnp.transpose(labels)
    group = lane_group((128, 128))
    lane = group.astype(F32)
    slab = lax.broadcasted_iota(jnp.int32, (256, 128), 0).astype(F32)
    total = None
    for step in range(16):
        slot = step % 2
        values = flat_ref[pl.ds(step, 128, stride=18), :]
        rolls = [values] + [pltpu.roll(values, 32 * j, 1) for j in range(1, 4)]
        for g in range(4):
            copies = rolls[(-g) % 4]
            for h in range(1, 4):
                copies = jnp.where(group == h, rolls[(h - g) % 4], copies)
            copies = copies.astype(BF16)
            tile = 16 * g + step
            place = jnp.broadcast_to(labels[:, 64 + tile : 65 + tile], (128, 128)) - lane
            place = place.astype(BF16)
            for m in range(4):
                spread_ref[slot, 128 * g : 128 * g + 128, 128 * m : 128 * m + 128] = jnp.where(
                    place == jnp.array(4.0 * m, BF16), copies, jnp.zeros_like(copies)
                )
            hot = jnp.broadcast_to(named[tile : tile + 1, :], (256, 128)) == slab
            hot_ref[slot, :, 128 * g : 128 * g + 128] = jnp.where(hot, 1.0, 0.0).astype(BF16)
        part = jnp.dot(hot_ref[slot], spread_ref[slot], preferred_element_type=F32)
        total = part if total is None else total + part
    total = total.astype(BF16)
    for core in range(2):
        for e in range(4):
            out_ref[4 * core + e] = total[128 * core : 128 * core + 128]


def rows_body(
    mix_ref, cells_ref, turn_ref, row_table_ref, slab_table_ref, phase_ref, out_ref, flat_ref
):
    halves = []
    for low in range(2):
        real, imag = [], []
        for core in range(2):
            parts = [
                cells_ref[4 * core + e, :, 256 * low : 256 * low + 256].astype(F32)
                for e in range(4)
            ]
            sum_real = parts[0] * mix_ref[0]
            sum_imag = -(parts[0] * mix_ref[4])
            for e in range(1, 4):
                sum_real = sum_real + parts[e] * mix_ref[e]
                sum_imag = sum_imag - parts[e] * mix_ref[4 + e]
            cosine = turn_ref[0:1, 256 * core : 256 * core + 256]
            sine = turn_ref[1:2, 256 * core : 256 * core + 256]
            real.append(sum_real * cosine + sum_imag * sine)
            imag.append(sum_imag * cosine - sum_real * sine)
        halves.append(jnp.concatenate(real + imag, 1).astype(BF16))
    spectrum = jnp.dot(
        jnp.concatenate(halves, 0), row_table_ref[...], preferred_element_type=F32
    ).astype(BF16)
    for low in range(2):
        half = spectrum[128 * low : 128 * low + 128]
        stacked = jnp.concatenate([half[:, :512], half[:, 512:]], 0)
        combined = jnp.dot(slab_table_ref[...], stacked, preferred_element_type=F32)
        cosine = phase_ref[:, 2 * low : 2 * low + 1]
        sine = phase_ref[:, 2 * low + 1 : 2 * low + 2]
        real, imag = combined[:128], combined[128:]
        turned = [real * cosine + imag * sine, imag * cosine - real * sine]
        for p in range(2):
            for v in range(4):
                flat_ref[pl.ds(4 * (2 * low + p) + v, 128, stride=16), :] = turned[p][
                    :, 128 * v : 128 * v + 128
                ]
    out_ref[...] = flat_ref[...].astype(BF16)


def final_body(rows_ref, table_ref, psf_ref, out_ref, flat_ref, values_ref, result_ref, sems):
    flat_ref[...] = rows_ref[...].astype(F32)
    for v in range(4):
        values_ref[:, 128 * v : 128 * v + 128] = flat_ref[pl.ds(v, 512, stride=4), :].astype(BF16)
    copies = []
    for part in range(4):
        start = 64 * part
        result = jnp.dot(
            table_ref[128 * part : 128 * part + 128, :],
            values_ref[...],
            preferred_element_type=F32,
        )
        psf = psf_ref[start : start + 64, :].astype(F32)
        result_ref[start : start + 64, 0, :] = result[:64] * psf
        result_ref[start : start + 64, 1, :] = result[64:] * psf
        window = pl.ds(start, 64)
        copy = pltpu.make_async_copy(result_ref.at[window], out_ref.at[window], sems.at[part])
        copy.start()
        copies.append(copy)
    for copy in copies:
        copy.wait()


VMEM = pl.BlockSpec(memory_space=pltpu.VMEM)
SMEM = pl.BlockSpec(memory_space=pltpu.SMEM)


def in_vmem(x):
    return pltpu.with_memory_space_constraint(x, pltpu.VMEM)


def on_device(tile_density, tile_dest, tile_place, psf_spectrum):
    chip = lax.axis_index("chip")
    core = lax.axis_index("core")
    me_col = lax.axis_index("cols")
    iota = lambda n: jnp.arange(n, dtype=jnp.int32)

    outgoing = pl.pallas_call(
        pack_body,
        in_specs=[VMEM] * 3,
        out_specs=VMEM,
        out_shape=jax.ShapeDtypeStruct((2304, 128), BF16),
        scratch_shapes=[pltpu.VMEM((2048, 128), F32), pltpu.VMEM((2304, 128), F32)],
    )(tile_density, tile_dest.reshape(1, 64), tile_place.reshape(1, 64))
    arrived = lax.all_to_all(outgoing.reshape(128, 9, 2, 128), ROWS, 0, 0, tiled=True)
    sent = pl.pallas_call(
        scatter_body,
        in_specs=[VMEM],
        out_specs=VMEM,
        out_shape=jax.ShapeDtypeStruct((8, 128, 512), BF16),
        scratch_shapes=[
            pltpu.VMEM((2304, 128), F32),
            pltpu.VMEM((2, 512, 512), BF16),
            pltpu.VMEM((2, 256, 512), BF16),
        ],
    )(in_vmem(arrived.reshape(2304, 128)))

    cells = lax.all_to_all(sent, GROUP, 0, 0, tiled=True)

    order = iota(512)
    column = order % 256 // 32 * 64 + order // 256 * 32 + order % 32
    cosine, sine = table_parts(
        column[:, None], iota(512)[None, :], 512, 1.0 / math.sqrt(2048)
    )
    row_table = jnp.concatenate(
        [jnp.concatenate([cosine, -sine], 1), jnp.concatenate([sine, cosine], 1)], 0
    ).astype(BF16)
    cosine, sine = table_parts(iota(128)[:, None], iota(128)[None, :], 128, 1.0)
    slab_table = jnp.concatenate(
        [jnp.concatenate([cosine, sine], 1), jnp.concatenate([-sine, cosine], 1)], 0
    ).astype(BF16)
    angles = 2.0 * math.pi / 4 * (iota(4) * me_col % 4).astype(F32)
    mix = jnp.concatenate([jnp.cos(angles), jnp.sin(angles)])
    turn = jnp.stack(twiddle_parts(column, me_col, 2048), 0)
    phases = []
    for low in range(2):
        phases += twiddle_parts(64 * (2 * core + low) + chip, iota(128), 32768)
    phase = jnp.stack(phases, 1)

    section_two = pl.pallas_call(
        rows_body,
        in_specs=[SMEM] + [VMEM] * 5,
        out_specs=VMEM,
        out_shape=jax.ShapeDtypeStruct((2048, 128), BF16),
        scratch_shapes=[pltpu.VMEM((2048, 128), F32)],
    )(
        mix,
        in_vmem(cells),
        in_vmem(turn),
        in_vmem(row_table),
        in_vmem(slab_table),
        in_vmem(phase),
    )
    section_two = lax.all_to_all(section_two.reshape(128, 16, 128), ROWS, 0, 0, tiled=True)

    place = iota(256)
    position = 64 * (place % 4) + place // 4
    cosine, sine = table_parts(
        iota(256)[:, None], position[None, :], 256, 1.0 / math.sqrt(32768)
    )
    real = jnp.stack([cosine, sine], 2).reshape(4, 1, 64, 512)
    imag = jnp.stack([-sine, cosine], 2).reshape(4, 1, 64, 512)
    final_table = jnp.concatenate([real, imag], 1).reshape(512, 512).astype(BF16)
    return pl.pallas_call(
        final_body,
        in_specs=[VMEM] * 3,
        out_specs=pl.BlockSpec(memory_space=pl.ANY),
        out_shape=jax.ShapeDtypeStruct((256, 2, 512), F32),
        scratch_shapes=[
            pltpu.VMEM((2048, 128), F32),
            pltpu.VMEM((512, 512), BF16),
            pltpu.VMEM((256, 2, 512), F32),
            pltpu.SemaphoreType.DMA((4,)),
        ],
    )(
        in_vmem(section_two.reshape(2048, 128)), in_vmem(final_table), in_vmem(psf_spectrum)
    )


def solution(mesh):
    split = Mesh(
        mesh.devices.reshape(mesh.devices.shape[0] // 2, 2, mesh.devices.shape[1]),
        ("chip", "core", "cols"),
    )
    everywhere = ("chip", "core", "cols")
    in_specs = (P(everywhere, None, None), P(everywhere, None), P(everywhere), P(ROWS, "cols"))
    return jax.shard_map(
        on_device,
        mesh=split,
        in_specs=in_specs,
        out_specs=P(ROWS, None, "cols"),
        check_vma=False,
    )
```

```python
import math

import jax
import jax.numpy as jnp
from jax import lax
from jax.experimental import pallas as pl
from jax.experimental.pallas import tpu as pltpu
from jax.sharding import Mesh
from jax.sharding import PartitionSpec as P

ROWS = ("chip", "core")
EVERYWHERE = ("chip", "core", "cols")
F32 = jnp.float32
BF16 = jnp.bfloat16


def cosines(index, period):
    return jnp.cos(2.0 * math.pi / period * (index % period).astype(F32))


def lane_group(shape):
    return lax.broadcasted_iota(jnp.int32, shape, 1) // 32


def pack_body(tiles_ref, dest_ref, place_ref, out_ref, flat_ref, packed_ref):
    for tile in range(32):
        start = 64 * tile
        flat_ref[start : start + 64, :64] = tiles_ref[tile].astype(F32)
        flat_ref[start : start + 64, 64:] = tiles_ref[tile + 32].astype(F32)
    place = place_ref[...]
    labels = jnp.concatenate([place // 16 * 128 + dest_ref[...], place % 16], 1).astype(F32)
    group = lax.broadcasted_iota(jnp.int32, (1, 128), 1) // 16
    swapped = jnp.where(
        group % 2 == 0, pltpu.roll(labels, 112, 1), pltpu.roll(labels, 16, 1)
    )
    labels = [jnp.broadcast_to(row, (2, 128)) for row in (labels, swapped)]
    odd = lane_group((16, 128)) % 2 == 1
    for chip in range(64):
        first = flat_ref[pl.ds(chip, 16, stride=64), :]
        second = flat_ref[pl.ds(1024 + chip, 16, stride=64), :]
        values = [
            jnp.where(odd, pltpu.roll(second, 32, 1), first),
            jnp.where(odd, first, pltpu.roll(second, 96, 1)),
        ]
        for core in range(2):
            start = 18 * (2 * chip + core)
            packed_ref[start : start + 16] = values[core]
            packed_ref[start + 16 : start + 18] = labels[core]
    out_ref[...] = packed_ref[...].astype(BF16)


def scatter_body(tiles_ref, order_ref, out_ref, flat_ref, spread_ref, hot_ref):
    flat_ref[...] = tiles_ref[...].astype(F32)
    labels = flat_ref[pl.ds(16, 128, stride=18), :]
    named = jnp.transpose(labels)
    group = lane_group((128, 128))
    lane = group.astype(F32)
    slab = lax.broadcasted_iota(jnp.int32, (256, 128), 0).astype(F32)
    total = None
    for step in range(16):
        slot = step % 2
        values = flat_ref[pl.ds(step, 128, stride=18), :]
        rolls = [values] + [pltpu.roll(values, 32 * j, 1) for j in range(1, 4)]
        for g in range(4):
            copies = rolls[(-g) % 4]
            for h in range(1, 4):
                copies = jnp.where(group == h, rolls[(h - g) % 4], copies)
            copies = copies.astype(BF16)
            tile = 16 * g + step
            place = jnp.broadcast_to(labels[:, 64 + tile : 65 + tile], (128, 128)) - lane
            place = place.astype(BF16)
            for m in range(4):
                spread_ref[slot, 128 * g : 128 * g + 128, 128 * m : 128 * m + 128] = jnp.where(
                    place == jnp.array(4.0 * m, BF16), copies, jnp.zeros_like(copies)
                )
            hot = jnp.broadcast_to(named[tile : tile + 1, :], (256, 128)) == slab
            hot_ref[slot, :, 128 * g : 128 * g + 128] = jnp.where(hot, 1.0, 0.0).astype(BF16)
        part = jnp.dot(hot_ref[slot], spread_ref[slot], preferred_element_type=F32)
        total = part if total is None else total + part
    total = jnp.dot(total.astype(BF16), order_ref[...], preferred_element_type=F32)
    for octet in range(4):
        out_ref[octet] = total[:, 128 * octet : 128 * octet + 128].astype(BF16)


def turned(first, second, sign):
    return first + sign * pltpu.roll(second, 64, 1)


def lane_sign(shape):
    lane = lax.broadcasted_iota(jnp.int32, shape, 1)
    return jnp.where(lane < 64, 1.0, -1.0)


def rows_body(cells_ref, mix_table_ref, slab_table_ref, phase_ref, out_ref, flat_ref):
    cells = jnp.concatenate([cells_ref[e] for e in range(4)], 1)
    spectrum = jnp.dot(cells, mix_table_ref[...], preferred_element_type=F32).astype(BF16)
    sign = lane_sign((128, 128))
    for r in range(4):
        start = 128 * (r // 2)
        values = spectrum[start : start + 128, 512 * (r % 2) : 512 * (r % 2) + 512]
        both = jnp.dot(slab_table_ref[...], values, preferred_element_type=F32)
        first, second = both[:128], both[128:]
        cosine, sine = phase_ref[:, r : r + 1], phase_ref[:, 4 + r : 5 + r]
        straight = first * cosine - second * sine
        crossed = second * cosine + first * sine
        for k in range(4):
            lanes = slice(128 * k, 128 * k + 128)
            flat_ref[pl.ds(4 * k + r, 128, stride=16), :] = turned(
                straight[:, lanes], crossed[:, lanes], sign
            )
    out_ref[...] = flat_ref[...].astype(BF16)


def final_body(
    rows_ref,
    table_ref,
    cell_table_hbm,
    psf_ref,
    out_ref,
    flat_ref,
    values_ref,
    cell_table_ref,
    result_ref,
    sems,
):
    fetch = pltpu.make_async_copy(cell_table_hbm, cell_table_ref, sems.at[2])
    fetch.start()
    flat_ref[...] = rows_ref[...].astype(F32)
    for h in range(8):
        for r in range(4):
            values_ref[64 * r : 64 * r + 64, 128 * h : 128 * h + 128] = flat_ref[
                pl.ds(4 * h + r, 64, stride=32), :
            ].astype(BF16)
    both = jnp.dot(table_ref[...], values_ref[...], preferred_element_type=F32)
    sign = lane_sign((256, 128))
    for h in range(8):
        lanes = slice(128 * h, 128 * h + 128)
        values_ref[:, lanes] = turned(both[:256, lanes], both[256:, lanes], sign).astype(BF16)
    fetch.wait()
    copies = []
    for part in range(2):
        window = pl.ds(128 * part, 128)
        result = jnp.dot(
            values_ref[window, :], cell_table_ref[...], preferred_element_type=F32
        )
        psf = psf_ref[window, :].astype(F32)
        result_ref[window, 0, :] = result[:, :512] * psf
        result_ref[window, 1, :] = result[:, 512:] * psf
        copy = pltpu.make_async_copy(result_ref.at[window], out_ref.at[window], sems.at[part])
        copy.start()
        copies.append(copy)
    for copy in copies:
        copy.wait()


VMEM = pl.BlockSpec(memory_space=pltpu.VMEM)


def in_vmem(x):
    return pltpu.with_memory_space_constraint(x, pltpu.VMEM)


def on_device(tile_density, tile_dest, tile_place, psf_spectrum):
    chip = lax.axis_index("chip")
    core = lax.axis_index("core")
    me_col = lax.axis_index("cols")
    iota = lambda n: jnp.arange(n, dtype=jnp.int32)

    member = 4 * core + me_col

    out = iota(512)
    source = out % 128 // 8 * 32 + out // 128 * 8 + out % 8
    order_table = (iota(512)[:, None] == source[None, :]).astype(BF16)

    given, out = iota(512)[:, None], iota(1024)[None, :]
    column = given // 128 * 512 + given % 64 // 8 * 64 + 8 * member + given % 8
    frequency = out % 512 // 128 + 4 * (out % 64 // 8)
    same = (given % 128 // 64 == out // 512) & (given % 8 == out % 8)
    mix_table = cosines(column * frequency + 512 * (out % 128 // 64), 2048)
    mix_table = jnp.where(same, mix_table * (1.0 / math.sqrt(2048)), 0.0).astype(BF16)

    given, out = iota(128)[None, :], iota(256)[:, None]
    slab_table = cosines(given * (out % 128) + 96 * (out // 128), 128).astype(BF16)
    part = iota(8)[None, :]
    phase = cosines(
        (64 * (part % 4) + chip) * iota(128)[:, None] + 24576 * (part // 4), 32768
    )

    given, out = iota(256)[None, :], iota(512)[:, None]
    final_table = cosines(given * (out % 256) + 192 * (out // 256), 256)
    final_table = (final_table * (1.0 / math.sqrt(32768))).astype(BF16)

    given, out = iota(1024)[:, None], iota(1024)[None, :]
    cell = given // 128 * 8 + given % 8
    turn = 16 * (out // 512 - given % 128 // 64)
    cell_table = cosines(cell * (out % 512 // 8) + turn + 64, 64)
    cell_table = jnp.where(given % 64 // 8 == out % 8, cell_table, 0.0).astype(BF16)

    outgoing = pl.pallas_call(
        pack_body,
        in_specs=[VMEM] * 3,
        out_specs=VMEM,
        out_shape=jax.ShapeDtypeStruct((2304, 128), BF16),
        scratch_shapes=[pltpu.VMEM((2048, 128), F32), pltpu.VMEM((2304, 128), F32)],
    )(tile_density, tile_dest.reshape(1, 64), tile_place.reshape(1, 64))
    arrived = lax.all_to_all(outgoing.reshape(128, 9, 2, 128), ROWS, 0, 0, tiled=True)
    arrived, order_table, mix_table, slab_table, phase, final_table, cell_table = (
        lax.optimization_barrier(
            (arrived, order_table, mix_table, slab_table, phase, final_table, cell_table)
        )
    )
    sent = pl.pallas_call(
        scatter_body,
        in_specs=[VMEM] * 2,
        out_specs=VMEM,
        out_shape=jax.ShapeDtypeStruct((4, 256, 128), BF16),
        scratch_shapes=[
            pltpu.VMEM((2304, 128), F32),
            pltpu.VMEM((2, 512, 512), BF16),
            pltpu.VMEM((2, 256, 512), BF16),
        ],
    )(in_vmem(arrived.reshape(2304, 128)), in_vmem(order_table))

    cells = lax.all_to_all(sent, "cols", 0, 0, tiled=True)
    section_two = pl.pallas_call(
        rows_body,
        in_specs=[VMEM] * 4,
        out_specs=VMEM,
        out_shape=jax.ShapeDtypeStruct((2048, 128), BF16),
        scratch_shapes=[pltpu.VMEM((2048, 128), F32)],
    )(in_vmem(cells), in_vmem(mix_table), in_vmem(slab_table), in_vmem(phase))

    section_two = lax.all_to_all(
        section_two.reshape(512, 2, 2, 128), EVERYWHERE, 0, 0, tiled=True
    )
    return pl.pallas_call(
        final_body,
        in_specs=[VMEM, VMEM, pl.BlockSpec(memory_space=pl.ANY), VMEM],
        out_specs=pl.BlockSpec(memory_space=pl.ANY),
        out_shape=jax.ShapeDtypeStruct((256, 2, 512), F32),
        scratch_shapes=[
            pltpu.VMEM((2048, 128), F32),
            pltpu.VMEM((256, 1024), BF16),
            pltpu.VMEM((1024, 1024), BF16),
            pltpu.VMEM((256, 2, 512), F32),
            pltpu.SemaphoreType.DMA((3,)),
        ],
    )(
        in_vmem(section_two.reshape(2048, 128)),
        in_vmem(final_table),
        cell_table,
        in_vmem(psf_spectrum),
    )


def solution(mesh):
    rows, cols = mesh.devices.shape
    split = Mesh(mesh.devices.reshape(rows // 2, 2, cols), EVERYWHERE)
    in_specs = (P(EVERYWHERE, None, None), P(EVERYWHERE, None), P(EVERYWHERE), P(ROWS, "cols"))
    return jax.shard_map(
        on_device,
        mesh=split,
        in_specs=in_specs,
        out_specs=P(ROWS, None, "cols"),
        check_vma=False,
    )
```

```python
import math

import jax
import jax.numpy as jnp
from jax import lax
from jax.experimental import pallas as pl
from jax.experimental.pallas import tpu as pltpu
from jax.sharding import Mesh
from jax.sharding import PartitionSpec as P

ROWS = ("chip", "core")
EVERYWHERE = ("chip", "core", "cols")
F32 = jnp.float32
BF16 = jnp.bfloat16


def cosines(index, period):
    return jnp.cos(2.0 * math.pi / period * (index % period).astype(F32))


def lane_group(shape):
    return lax.broadcasted_iota(jnp.int32, shape, 1) // 32


def pack_body(tiles_ref, dest_ref, place_ref, out_ref, flat_ref, packed_ref):
    for tile in range(32):
        start = 64 * tile
        flat_ref[start : start + 64, :64] = tiles_ref[tile].astype(F32)
        flat_ref[start : start + 64, 64:] = tiles_ref[tile + 32].astype(F32)
    place = place_ref[...]
    labels = jnp.concatenate([place // 16 * 128 + dest_ref[...], place % 16], 1).astype(F32)
    group = lax.broadcasted_iota(jnp.int32, (1, 128), 1) // 16
    swapped = jnp.where(
        group % 2 == 0, pltpu.roll(labels, 112, 1), pltpu.roll(labels, 16, 1)
    )
    labels = [jnp.broadcast_to(row, (2, 128)) for row in (labels, swapped)]
    odd = lane_group((16, 128)) % 2 == 1
    for chip in range(64):
        first = flat_ref[pl.ds(chip, 16, stride=64), :]
        second = flat_ref[pl.ds(1024 + chip, 16, stride=64), :]
        values = [
            jnp.where(odd, pltpu.roll(second, 32, 1), first),
            jnp.where(odd, first, pltpu.roll(second, 96, 1)),
        ]
        for core in range(2):
            start = 18 * (2 * chip + core)
            packed_ref[start : start + 16] = values[core]
            packed_ref[start + 16 : start + 18] = labels[core]
    out_ref[...] = packed_ref[...].astype(BF16)


def scatter_body(tiles_ref, order_ref, out_ref, flat_ref, spread_ref, hot_ref):
    flat_ref[...] = tiles_ref[...].astype(F32)
    labels = flat_ref[pl.ds(16, 128, stride=18), :]
    named = jnp.transpose(labels)
    group = lane_group((128, 128))
    lane = group.astype(F32)
    slab = lax.broadcasted_iota(jnp.int32, (256, 128), 0).astype(F32)
    total = None
    for step in range(16):
        slot = step % 2
        values = flat_ref[pl.ds(step, 128, stride=18), :]
        rolls = [values] + [pltpu.roll(values, 32 * j, 1) for j in range(1, 4)]
        for g in range(4):
            copies = rolls[(-g) % 4]
            for h in range(1, 4):
                copies = jnp.where(group == h, rolls[(h - g) % 4], copies)
            copies = copies.astype(BF16)
            tile = 16 * g + step
            place = jnp.broadcast_to(labels[:, 64 + tile : 65 + tile], (128, 128)) - lane
            place = place.astype(BF16)
            for m in range(4):
                spread_ref[slot, 128 * g : 128 * g + 128, 128 * m : 128 * m + 128] = jnp.where(
                    place == jnp.array(4.0 * m, BF16), copies, jnp.zeros_like(copies)
                )
            hot = jnp.broadcast_to(named[tile : tile + 1, :], (256, 128)) == slab
            hot_ref[slot, :, 128 * g : 128 * g + 128] = jnp.where(hot, 1.0, 0.0).astype(BF16)
        part = jnp.dot(hot_ref[slot], spread_ref[slot], preferred_element_type=F32)
        total = part if total is None else total + part
    total = jnp.dot(total.astype(BF16), order_ref[...], preferred_element_type=F32)
    for octet in range(4):
        out_ref[octet] = total[:, 128 * octet : 128 * octet + 128].astype(BF16)


def lane_sign(shape):
    lane = lax.broadcasted_iota(jnp.int32, shape, 1)
    return jnp.where(lane < 64, 1.0, -1.0)


def rows_body(cells_ref, mix_table_ref, slab_table_ref, phase_ref, out_ref, flat_ref):
    sign = lane_sign((128, 128))
    left = lax.broadcasted_iota(jnp.int32, (256, 128), 1) < 64
    for low in range(2):
        pairs = []
        for e in (0, 2):
            first, second = cells_ref[e].astype(F32), cells_ref[e + 1].astype(F32)
            if low == 0:
                second = pltpu.roll(second, 64, 1)
            else:
                first = pltpu.roll(first, 64, 1)
            pairs.append(jnp.where(left, first, second).astype(BF16))
        spectrum = jnp.dot(
            jnp.concatenate(pairs, 1), mix_table_ref[...], preferred_element_type=F32
        ).astype(BF16)
        for half in range(2):
            r = 2 * half + low
            values = spectrum[128 * half : 128 * half + 128]
            both = jnp.dot(slab_table_ref[...], values, preferred_element_type=F32)
            first, second = both[:128], both[128:]
            cosine, sine = phase_ref[:, r : r + 1], phase_ref[:, 4 + r : 5 + r]
            straight = first * cosine - second * sine
            crossed = second * cosine + first * sine
            for k in range(4):
                lanes = slice(128 * k, 128 * k + 128)
                flat_ref[pl.ds(4 * k + r, 128, stride=16), :] = straight[
                    :, lanes
                ] + sign * pltpu.roll(crossed[:, lanes], 64, 1)
    out_ref[...] = flat_ref[...].astype(BF16)


def final_body(
    rows_ref,
    table_ref,
    cell_table_hbm,
    psf_ref,
    out_ref,
    flat_ref,
    values_ref,
    cell_table_ref,
    stacked_ref,
    result_ref,
    sems,
):
    fetch = pltpu.make_async_copy(cell_table_hbm, cell_table_ref, sems.at[4])
    fetch.start()
    flat_ref[...] = rows_ref[...].astype(F32)
    for h in range(8):
        for r in range(4):
            values_ref[64 * r : 64 * r + 64, 128 * h : 128 * h + 128] = flat_ref[
                pl.ds(4 * h + r, 64, stride=32), :
            ].astype(BF16)
    fetch.wait()
    spectrum = jnp.dot(values_ref[...], cell_table_ref[...], preferred_element_type=F32)
    stacked_ref[:256] = spectrum[:, :512].astype(BF16)
    stacked_ref[256:] = spectrum[:, 512:].astype(BF16)
    copies = []
    for part in range(4):
        window = pl.ds(64 * part, 64)
        result = jnp.dot(
            table_ref[128 * part : 128 * part + 128, :],
            stacked_ref[...],
            preferred_element_type=F32,
        )
        psf = psf_ref[window, :].astype(F32)
        result_ref[window, 0, :] = result[:64] * psf
        result_ref[window, 1, :] = result[64:] * psf
        copy = pltpu.make_async_copy(result_ref.at[window], out_ref.at[window], sems.at[part])
        copy.start()
        copies.append(copy)
    for copy in copies:
        copy.wait()


VMEM = pl.BlockSpec(memory_space=pltpu.VMEM)


def in_vmem(x):
    return pltpu.with_memory_space_constraint(x, pltpu.VMEM)


def on_device(tile_density, tile_dest, tile_place, psf_spectrum):
    chip = lax.axis_index("chip")
    core = lax.axis_index("core")
    me_col = lax.axis_index("cols")
    iota = lambda n: jnp.arange(n, dtype=jnp.int32)

    member = 4 * core + me_col

    out = iota(512)
    source = out % 128 // 8 * 32 + out // 128 * 8 + out % 8
    order_table = (iota(512)[:, None] == source[None, :]).astype(BF16)

    given, out = iota(256)[:, None], iota(512)[None, :]
    column = given // 8 * 64 + 8 * member + given % 8
    frequency = out // 128 + 4 * (out % 64 // 8)
    mix_table = cosines(column * frequency + 512 * (out % 128 // 64), 2048)
    mix_table = jnp.where(
        given % 8 == out % 8, mix_table * (1.0 / math.sqrt(2048)), 0.0
    ).astype(BF16)

    given, out = iota(128)[None, :], iota(256)[:, None]
    slab_table = cosines(given * (out % 128) + 96 * (out // 128), 128).astype(BF16)
    part = iota(8)[None, :]
    phase = cosines(
        (64 * (part % 4) + chip) * iota(128)[:, None] + 24576 * (part // 4), 32768
    )

    given, out = iota(512)[None, :], iota(512)[:, None]
    frequency = out // 128 * 64 + out % 64
    turn = 64 * (out % 128 // 64) - 64 * (given // 256) + 256
    final_table = cosines(given % 256 * frequency + turn, 256)
    final_table = (final_table * (1.0 / math.sqrt(32768))).astype(BF16)

    given, out = iota(128)[:, None], iota(128)[None, :]
    turn = 16 * (out // 64 - given % 16 // 8) + 64
    cell_table = cosines((given // 16 * 8 + given % 8) * (out % 64) + turn, 64).astype(BF16)
    given, out = iota(1024)[:, None], iota(1024)[None, :]
    from_rows = given // 64 * 8 + given % 8 == iota(128)[None, :]
    to_columns = iota(128)[:, None] == out // 8
    cell_table = jnp.dot(from_rows.astype(BF16), cell_table)
    cell_table = jnp.dot(cell_table, to_columns.astype(BF16))
    cell_table = jnp.where(given % 64 // 8 == out % 8, cell_table, jnp.zeros_like(cell_table))

    outgoing = pl.pallas_call(
        pack_body,
        in_specs=[VMEM] * 3,
        out_specs=VMEM,
        out_shape=jax.ShapeDtypeStruct((2304, 128), BF16),
        scratch_shapes=[pltpu.VMEM((2048, 128), F32), pltpu.VMEM((2304, 128), F32)],
    )(tile_density, tile_dest.reshape(1, 64), tile_place.reshape(1, 64))
    arrived = lax.all_to_all(outgoing.reshape(128, 9, 2, 128), ROWS, 0, 0, tiled=True)
    arrived, order_table, mix_table, slab_table, phase, final_table, cell_table = (
        lax.optimization_barrier(
            (arrived, order_table, mix_table, slab_table, phase, final_table, cell_table)
        )
    )
    sent = pl.pallas_call(
        scatter_body,
        in_specs=[VMEM] * 2,
        out_specs=VMEM,
        out_shape=jax.ShapeDtypeStruct((4, 256, 128), BF16),
        scratch_shapes=[
            pltpu.VMEM((2304, 128), F32),
            pltpu.VMEM((2, 512, 512), BF16),
            pltpu.VMEM((2, 256, 512), BF16),
        ],
    )(in_vmem(arrived.reshape(2304, 128)), in_vmem(order_table))

    cells = lax.all_to_all(sent, "cols", 0, 0, tiled=True)
    section_two = pl.pallas_call(
        rows_body,
        in_specs=[VMEM] * 4,
        out_specs=VMEM,
        out_shape=jax.ShapeDtypeStruct((2048, 128), BF16),
        scratch_shapes=[pltpu.VMEM((2048, 128), F32)],
    )(in_vmem(cells), in_vmem(mix_table), in_vmem(slab_table), in_vmem(phase))

    section_two = lax.all_to_all(
        section_two.reshape(512, 2, 2, 128), EVERYWHERE, 0, 0, tiled=True
    )
    return pl.pallas_call(
        final_body,
        in_specs=[VMEM, VMEM, pl.BlockSpec(memory_space=pl.ANY), VMEM],
        out_specs=pl.BlockSpec(memory_space=pl.ANY),
        out_shape=jax.ShapeDtypeStruct((256, 2, 512), F32),
        scratch_shapes=[
            pltpu.VMEM((2048, 128), F32),
            pltpu.VMEM((256, 1024), BF16),
            pltpu.VMEM((1024, 1024), BF16),
            pltpu.VMEM((512, 512), BF16),
            pltpu.VMEM((256, 2, 512), F32),
            pltpu.SemaphoreType.DMA((5,)),
        ],
    )(
        in_vmem(section_two.reshape(2048, 128)),
        in_vmem(final_table),
        cell_table,
        in_vmem(psf_spectrum),
    )


def solution(mesh):
    rows, cols = mesh.devices.shape
    split = Mesh(mesh.devices.reshape(rows // 2, 2, cols), EVERYWHERE)
    in_specs = (P(EVERYWHERE, None, None), P(EVERYWHERE, None), P(EVERYWHERE), P(ROWS, "cols"))
    return jax.shard_map(
        on_device,
        mesh=split,
        in_specs=in_specs,
        out_specs=P(ROWS, None, "cols"),
        check_vma=False,
    )
```

```python
import math

import jax
import jax.numpy as jnp
from jax import lax
from jax.experimental import pallas as pl
from jax.experimental.pallas import tpu as pltpu
from jax.sharding import Mesh
from jax.sharding import PartitionSpec as P

ROWS = ("chip", "core")
EVERYWHERE = ("chip", "core", "cols")
F32 = jnp.float32
BF16 = jnp.bfloat16


def cosines(index, period):
    return jnp.cos(2.0 * math.pi / period * (index % period).astype(F32))


def lane_group(shape):
    return lax.broadcasted_iota(jnp.int32, shape, 1) // 32


def pack_body(tiles_ref, dest_ref, place_ref, out_ref, flat_ref, packed_ref):
    for tile in range(32):
        start = 64 * tile
        flat_ref[start : start + 64, :64] = tiles_ref[tile].astype(F32)
        flat_ref[start : start + 64, 64:] = tiles_ref[tile + 32].astype(F32)
    place = place_ref[...]
    labels = jnp.concatenate([place // 16 * 128 + dest_ref[...], place % 16], 1).astype(F32)
    group = lax.broadcasted_iota(jnp.int32, (1, 128), 1) // 16
    swapped = jnp.where(
        group % 2 == 0, pltpu.roll(labels, 112, 1), pltpu.roll(labels, 16, 1)
    )
    labels = [jnp.broadcast_to(row, (2, 128)) for row in (labels, swapped)]
    odd = lane_group((16, 128)) % 2 == 1
    for chip in range(64):
        first = flat_ref[pl.ds(chip, 16, stride=64), :]
        second = flat_ref[pl.ds(1024 + chip, 16, stride=64), :]
        values = [
            jnp.where(odd, pltpu.roll(second, 32, 1), first),
            jnp.where(odd, first, pltpu.roll(second, 96, 1)),
        ]
        for core in range(2):
            start = 18 * (2 * chip + core)
            packed_ref[start : start + 16] = values[core]
            packed_ref[start + 16 : start + 18] = labels[core]
    out_ref[...] = packed_ref[...].astype(BF16)


def scatter_body(tiles_ref, out_ref, flat_ref, spread_ref, hot_ref):
    flat_ref[...] = tiles_ref[...].astype(F32)
    labels = flat_ref[pl.ds(16, 128, stride=18), :]
    named = jnp.transpose(labels)
    group = lane_group((128, 128))
    lane = group.astype(F32)
    slab = lax.broadcasted_iota(jnp.int32, (256, 128), 0).astype(F32)
    total = None
    for step in range(16):
        slot = step % 2
        values = flat_ref[pl.ds(step, 128, stride=18), :]
        rolls = [values] + [pltpu.roll(values, 32 * j, 1) for j in range(1, 4)]
        for g in range(4):
            copies = rolls[(-g) % 4]
            for h in range(1, 4):
                copies = jnp.where(group == h, rolls[(h - g) % 4], copies)
            copies = copies.astype(BF16)
            tile = 16 * g + step
            place = jnp.broadcast_to(labels[:, 64 + tile : 65 + tile], (128, 128)) - lane
            place = place.astype(BF16)
            for m in range(4):
                spread_ref[slot, 128 * g : 128 * g + 128, 128 * m : 128 * m + 128] = jnp.where(
                    place == jnp.array(4.0 * m, BF16), copies, jnp.zeros_like(copies)
                )
            hot = jnp.broadcast_to(named[tile : tile + 1, :], (256, 128)) == slab
            hot_ref[slot, :, 128 * g : 128 * g + 128] = jnp.where(hot, 1.0, 0.0).astype(BF16)
        part = jnp.dot(hot_ref[slot], spread_ref[slot], preferred_element_type=F32)
        total = part if total is None else total + part
    total = total.astype(BF16)
    lane = lax.broadcasted_iota(jnp.int32, (512, 128), 1)
    source = lane // 8 * 32 + lane % 8
    given = lax.broadcasted_iota(jnp.int32, (512, 128), 0)
    for octet in range(4):
        order = jnp.where(given == source + 8 * octet, 1.0, 0.0).astype(BF16)
        out_ref[octet] = jnp.dot(total, order, preferred_element_type=F32).astype(BF16)


def lane_sign(shape):
    lane = lax.broadcasted_iota(jnp.int32, shape, 1)
    return jnp.where(lane < 64, 1.0, -1.0)


def rows_body(cells_ref, mix_table_ref, slab_table_ref, phase_ref, out_ref, flat_ref):
    sign = lane_sign((128, 128))
    left = lax.broadcasted_iota(jnp.int32, (256, 128), 1) < 64
    for low in range(2):
        pairs = []
        for e in (0, 2):
            first, second = cells_ref[e].astype(F32), cells_ref[e + 1].astype(F32)
            if low == 0:
                second = pltpu.roll(second, 64, 1)
            else:
                first = pltpu.roll(first, 64, 1)
            pairs.append(jnp.where(left, first, second).astype(BF16))
        spectrum = jnp.dot(
            jnp.concatenate(pairs, 1), mix_table_ref[...], preferred_element_type=F32
        ).astype(BF16)
        for half in range(2):
            r = 2 * half + low
            values = spectrum[128 * half : 128 * half + 128]
            both = jnp.dot(slab_table_ref[...], values, preferred_element_type=F32)
            first, second = both[:128], both[128:]
            cosine, sine = phase_ref[:, r : r + 1], phase_ref[:, 4 + r : 5 + r]
            straight = first * cosine - second * sine
            crossed = second * cosine + first * sine
            for k in range(4):
                lanes = slice(128 * k, 128 * k + 128)
                flat_ref[pl.ds(4 * k + r, 128, stride=16), :] = straight[
                    :, lanes
                ] + sign * pltpu.roll(crossed[:, lanes], 64, 1)
    out_ref[...] = flat_ref[...].astype(BF16)


def final_body(
    rows_ref,
    table_ref,
    cell_table_ref,
    psf_ref,
    out_ref,
    flat_ref,
    values_ref,
    stacked_ref,
    result_ref,
    sems,
):
    flat_ref[...] = rows_ref[...].astype(F32)
    for h in range(8):
        for r in range(4):
            values_ref[64 * r : 64 * r + 64, 128 * h : 128 * h + 128] = flat_ref[
                pl.ds(4 * h + r, 64, stride=32), :
            ].astype(BF16)
    spectrum = jnp.dot(values_ref[...], cell_table_ref[...], preferred_element_type=F32)
    stacked_ref[:256] = spectrum[:, :512].astype(BF16)
    stacked_ref[256:] = spectrum[:, 512:].astype(BF16)
    copies = []
    for part in range(4):
        window = pl.ds(64 * part, 64)
        result = jnp.dot(
            table_ref[128 * part : 128 * part + 128, :],
            stacked_ref[...],
            preferred_element_type=F32,
        )
        psf = psf_ref[window, :].astype(F32)
        result_ref[window, 0, :] = result[:64] * psf
        result_ref[window, 1, :] = result[64:] * psf
        copy = pltpu.make_async_copy(result_ref.at[window], out_ref.at[window], sems.at[part])
        copy.start()
        copies.append(copy)
    for copy in copies:
        copy.wait()


VMEM = pl.BlockSpec(memory_space=pltpu.VMEM)
GRANT = pltpu.CompilerParams(vmem_limit_bytes=16 * 2**20)


def in_vmem(x):
    return pltpu.with_memory_space_constraint(x, pltpu.VMEM)


def on_device(tile_density, tile_dest, tile_place, psf_spectrum):
    chip = lax.axis_index("chip")
    core = lax.axis_index("core")
    me_col = lax.axis_index("cols")
    iota = lambda n: jnp.arange(n, dtype=jnp.int32)

    member = 4 * core + me_col

    given, out = iota(256)[:, None], iota(512)[None, :]
    column = given // 8 * 64 + 8 * member + given % 8
    frequency = out // 128 + 4 * (out % 64 // 8)
    mix_table = cosines(column * frequency + 512 * (out % 128 // 64), 2048)
    mix_table = jnp.where(
        given % 8 == out % 8, mix_table * (1.0 / math.sqrt(2048)), 0.0
    ).astype(BF16)

    given, out = iota(128)[None, :], iota(256)[:, None]
    slab_table = cosines(given * (out % 128) + 96 * (out // 128), 128).astype(BF16)
    part = iota(8)[None, :]
    phase = cosines(
        (64 * (part % 4) + chip) * iota(128)[:, None] + 24576 * (part // 4), 32768
    )

    given, out = iota(512)[None, :], iota(512)[:, None]
    frequency = out // 128 * 64 + out % 64
    turn = 64 * (out % 128 // 64) - 64 * (given // 256) + 256
    final_table = cosines(given % 256 * frequency + turn, 256)
    final_table = (final_table * (1.0 / math.sqrt(32768))).astype(BF16)

    given, out = iota(128)[:, None], iota(128)[None, :]
    turn = 16 * (out // 64 - given % 16 // 8) + 64
    cell_table = cosines((given // 16 * 8 + given % 8) * (out % 64) + turn, 64).astype(BF16)
    given, out = iota(1024)[:, None], iota(1024)[None, :]
    from_rows = given // 64 * 8 + given % 8 == iota(128)[None, :]
    to_columns = iota(128)[:, None] == out // 8
    cell_table = jnp.dot(from_rows.astype(BF16), cell_table)
    cell_table = jnp.dot(cell_table, to_columns.astype(BF16))
    cell_table = jnp.where(given % 64 // 8 == out % 8, cell_table, jnp.zeros_like(cell_table))

    outgoing = pl.pallas_call(
        pack_body,
        in_specs=[VMEM] * 3,
        out_specs=VMEM,
        out_shape=jax.ShapeDtypeStruct((2304, 128), BF16),
        scratch_shapes=[pltpu.VMEM((2048, 128), F32), pltpu.VMEM((2304, 128), F32)],
    )(tile_density, tile_dest.reshape(1, 64), tile_place.reshape(1, 64))
    arrived = lax.all_to_all(outgoing.reshape(128, 9, 2, 128), ROWS, 0, 0, tiled=True)
    arrived, mix_table, slab_table, phase, final_table, cell_table = (
        lax.optimization_barrier(
            (arrived, mix_table, slab_table, phase, final_table, cell_table)
        )
    )
    sent = pl.pallas_call(
        scatter_body,
        in_specs=[VMEM],
        out_specs=VMEM,
        out_shape=jax.ShapeDtypeStruct((4, 256, 128), BF16),
        compiler_params=GRANT,
        scratch_shapes=[
            pltpu.VMEM((2304, 128), F32),
            pltpu.VMEM((2, 512, 512), BF16),
            pltpu.VMEM((2, 256, 512), BF16),
        ],
    )(in_vmem(arrived.reshape(2304, 128)))

    cells = lax.all_to_all(sent, "cols", 0, 0, tiled=True)
    section_two = pl.pallas_call(
        rows_body,
        in_specs=[VMEM] * 4,
        out_specs=VMEM,
        out_shape=jax.ShapeDtypeStruct((2048, 128), BF16),
        compiler_params=GRANT,
        scratch_shapes=[pltpu.VMEM((2048, 128), F32)],
    )(in_vmem(cells), in_vmem(mix_table), in_vmem(slab_table), in_vmem(phase))

    section_two = lax.all_to_all(
        section_two.reshape(512, 2, 2, 128), EVERYWHERE, 0, 0, tiled=True
    )
    return pl.pallas_call(
        final_body,
        in_specs=[VMEM] * 4,
        out_specs=pl.BlockSpec(memory_space=pl.ANY),
        out_shape=jax.ShapeDtypeStruct((256, 2, 512), F32),
        compiler_params=GRANT,
        scratch_shapes=[
            pltpu.VMEM((2048, 128), F32),
            pltpu.VMEM((256, 1024), BF16),
            pltpu.VMEM((512, 512), BF16),
            pltpu.VMEM((256, 2, 512), F32),
            pltpu.SemaphoreType.DMA((4,)),
        ],
    )(
        in_vmem(section_two.reshape(2048, 128)),
        in_vmem(final_table),
        in_vmem(cell_table),
        in_vmem(psf_spectrum),
    )


def solution(mesh):
    rows, cols = mesh.devices.shape
    split = Mesh(mesh.devices.reshape(rows // 2, 2, cols), EVERYWHERE)
    in_specs = (P(EVERYWHERE, None, None), P(EVERYWHERE, None), P(EVERYWHERE), P(ROWS, "cols"))
    return jax.shard_map(
        on_device,
        mesh=split,
        in_specs=in_specs,
        out_specs=P(ROWS, None, "cols"),
        check_vma=False,
    )
```

```python
import math

import jax
import jax.numpy as jnp
from jax import lax
from jax.experimental import pallas as pl
from jax.experimental.pallas import tpu as pltpu
from jax.sharding import Mesh
from jax.sharding import PartitionSpec as P

ROWS = ("chip", "core")
EVERYWHERE = ("chip", "core", "cols")
F32 = jnp.float32
BF16 = jnp.bfloat16


def cosines(index, period):
    return jnp.cos(2.0 * math.pi / period * (index % period).astype(F32))


def lane_group(shape):
    return lax.broadcasted_iota(jnp.int32, shape, 1) // 32


def pack_body(tiles_ref, dest_ref, place_ref, out_ref, flat_ref, packed_ref):
    for tile in range(32):
        start = 64 * tile
        flat_ref[start : start + 64, :64] = tiles_ref[tile].astype(F32)
        flat_ref[start : start + 64, 64:] = tiles_ref[tile + 32].astype(F32)
    place = place_ref[...]
    labels = jnp.concatenate([place // 16 * 128 + dest_ref[...], place % 16], 1).astype(F32)
    group = lax.broadcasted_iota(jnp.int32, (1, 128), 1) // 16
    swapped = jnp.where(
        group % 2 == 0, pltpu.roll(labels, 112, 1), pltpu.roll(labels, 16, 1)
    )
    labels = [jnp.broadcast_to(row, (2, 128)) for row in (labels, swapped)]
    odd = lane_group((16, 128)) % 2 == 1
    for chip in range(64):
        first = flat_ref[pl.ds(chip, 16, stride=64), :]
        second = flat_ref[pl.ds(1024 + chip, 16, stride=64), :]
        values = [
            jnp.where(odd, pltpu.roll(second, 32, 1), first),
            jnp.where(odd, first, pltpu.roll(second, 96, 1)),
        ]
        for core in range(2):
            start = 18 * (2 * chip + core)
            packed_ref[start : start + 16] = values[core]
            packed_ref[start + 16 : start + 18] = labels[core]
    out_ref[...] = packed_ref[...].astype(BF16)


def scatter_body(tiles_ref, out_ref, flat_ref, spread_ref, hot_ref):
    flat_ref[...] = tiles_ref[...].astype(F32)
    labels = flat_ref[pl.ds(16, 128, stride=18), :]
    named = jnp.transpose(labels)
    group = lane_group((128, 128))
    lane = group.astype(F32)
    slab = lax.broadcasted_iota(jnp.int32, (256, 128), 0).astype(F32)
    total = None
    for step in range(16):
        slot = step % 2
        values = flat_ref[pl.ds(step, 128, stride=18), :]
        rolls = [values] + [pltpu.roll(values, 32 * j, 1) for j in range(1, 4)]
        for g in range(4):
            copies = rolls[(-g) % 4]
            for h in range(1, 4):
                copies = jnp.where(group == h, rolls[(h - g) % 4], copies)
            copies = copies.astype(BF16)
            tile = 16 * g + step
            place = jnp.broadcast_to(labels[:, 64 + tile : 65 + tile], (128, 128)) - lane
            place = place.astype(BF16)
            for m in range(4):
                spread_ref[slot, 128 * g : 128 * g + 128, 128 * m : 128 * m + 128] = jnp.where(
                    place == jnp.array(4.0 * m, BF16), copies, jnp.zeros_like(copies)
                )
            hot = jnp.broadcast_to(named[tile : tile + 1, :], (256, 128)) == slab
            hot_ref[slot, :, 128 * g : 128 * g + 128] = jnp.where(hot, 1.0, 0.0).astype(BF16)
        part = jnp.dot(hot_ref[slot], spread_ref[slot], preferred_element_type=F32)
        total = part if total is None else total + part
    total = total.astype(BF16)
    lane = lax.broadcasted_iota(jnp.int32, (512, 128), 1)
    source = lane // 8 * 32 + lane % 8
    given = lax.broadcasted_iota(jnp.int32, (512, 128), 0)
    for octet in range(4):
        order = jnp.where(given == source + 8 * octet, 1.0, 0.0).astype(BF16)
        out_ref[octet] = jnp.dot(total, order, preferred_element_type=F32).astype(BF16)


def lane_sign(shape):
    lane = lax.broadcasted_iota(jnp.int32, shape, 1)
    return jnp.where(lane < 64, 1.0, -1.0)


def rows_body(
    cells_ref, mix_table_ref, slab_table_hbm, phase_ref, out_ref, flat_ref, slab_table_ref, sem
):
    fetch = pltpu.make_async_copy(slab_table_hbm, slab_table_ref, sem)
    fetch.start()
    sign = lane_sign((128, 128))
    left = lax.broadcasted_iota(jnp.int32, (256, 128), 1) < 64
    for low in range(2):
        pairs = []
        for e in (0, 2):
            first, second = cells_ref[e].astype(F32), cells_ref[e + 1].astype(F32)
            if low == 0:
                second = pltpu.roll(second, 64, 1)
            else:
                first = pltpu.roll(first, 64, 1)
            pairs.append(jnp.where(left, first, second).astype(BF16))
        spectrum = jnp.dot(
            jnp.concatenate(pairs, 1), mix_table_ref[...], preferred_element_type=F32
        ).astype(BF16)
        if low == 0:
            fetch.wait()
        for half in range(2):
            r = 2 * half + low
            values = spectrum[128 * half : 128 * half + 128]
            both = jnp.dot(slab_table_ref[...], values, preferred_element_type=F32)
            first, second = both[:128], both[128:]
            cosine, sine = phase_ref[:, r : r + 1], phase_ref[:, 4 + r : 5 + r]
            straight = first * cosine - second * sine
            crossed = second * cosine + first * sine
            for k in range(4):
                lanes = slice(128 * k, 128 * k + 128)
                flat_ref[pl.ds(4 * k + r, 128, stride=16), :] = straight[
                    :, lanes
                ] + sign * pltpu.roll(crossed[:, lanes], 64, 1)
    out_ref[...] = flat_ref[...].astype(BF16)


def final_body(
    rows_ref,
    table_ref,
    cell_table_ref,
    psf_ref,
    out_ref,
    flat_ref,
    values_ref,
    stacked_ref,
    result_ref,
    sems,
):
    flat_ref[...] = rows_ref[...].astype(F32)
    for h in range(8):
        for r in range(4):
            values_ref[64 * r : 64 * r + 64, 128 * h : 128 * h + 128] = flat_ref[
                pl.ds(4 * h + r, 64, stride=32), :
            ].astype(BF16)
    spectrum = jnp.dot(values_ref[...], cell_table_ref[...], preferred_element_type=F32)
    stacked_ref[:256] = spectrum[:, :512].astype(BF16)
    stacked_ref[256:] = spectrum[:, 512:].astype(BF16)
    copies = []
    for part in range(4):
        window = pl.ds(64 * part, 64)
        result = jnp.dot(
            table_ref[128 * part : 128 * part + 128, :],
            stacked_ref[...],
            preferred_element_type=F32,
        )
        psf = psf_ref[window, :].astype(F32)
        result_ref[window, 0, :] = result[:64] * psf
        result_ref[window, 1, :] = result[64:] * psf
        copy = pltpu.make_async_copy(result_ref.at[window], out_ref.at[window], sems.at[part])
        copy.start()
        copies.append(copy)
    for copy in copies:
        copy.wait()


VMEM = pl.BlockSpec(memory_space=pltpu.VMEM)
GRANT = pltpu.CompilerParams(vmem_limit_bytes=16 * 2**20)


def in_vmem(x):
    return pltpu.with_memory_space_constraint(x, pltpu.VMEM)


def on_device(tile_density, tile_dest, tile_place, psf_spectrum):
    chip = lax.axis_index("chip")
    core = lax.axis_index("core")
    me_col = lax.axis_index("cols")
    iota = lambda n: jnp.arange(n, dtype=jnp.int32)

    member = 4 * core + me_col

    given, out = iota(256)[:, None], iota(512)[None, :]
    column = given // 8 * 64 + 8 * member + given % 8
    frequency = out // 128 + 4 * (out % 64 // 8)
    mix_table = cosines(column * frequency + 512 * (out % 128 // 64), 2048)
    mix_table = jnp.where(
        given % 8 == out % 8, mix_table * (1.0 / math.sqrt(2048)), 0.0
    ).astype(BF16)

    given, out = iota(128)[None, :], iota(256)[:, None]
    slab_table = cosines(given * (out % 128) + 96 * (out // 128), 128).astype(BF16)
    part = iota(8)[None, :]
    phase = cosines(
        (64 * (part % 4) + chip) * iota(128)[:, None] + 24576 * (part // 4), 32768
    )

    given, out = iota(512)[None, :], iota(512)[:, None]
    frequency = out // 128 * 64 + out % 64
    turn = 64 * (out % 128 // 64) - 64 * (given // 256) + 256
    final_table = cosines(given % 256 * frequency + turn, 256)
    final_table = (final_table * (1.0 / math.sqrt(32768))).astype(BF16)

    given, out = iota(128)[:, None], iota(128)[None, :]
    turn = 16 * (out // 64 - given % 16 // 8) + 64
    cell_table = cosines((given // 16 * 8 + given % 8) * (out % 64) + turn, 64).astype(BF16)
    given, out = iota(1024)[:, None], iota(1024)[None, :]
    from_rows = given // 64 * 8 + given % 8 == iota(128)[None, :]
    to_columns = iota(128)[:, None] == out // 8
    cell_table = jnp.dot(from_rows.astype(BF16), cell_table)
    cell_table = jnp.dot(cell_table, to_columns.astype(BF16))
    cell_table = jnp.where(given % 64 // 8 == out % 8, cell_table, jnp.zeros_like(cell_table))

    outgoing = pl.pallas_call(
        pack_body,
        in_specs=[VMEM] * 3,
        out_specs=VMEM,
        out_shape=jax.ShapeDtypeStruct((2304, 128), BF16),
        scratch_shapes=[pltpu.VMEM((2048, 128), F32), pltpu.VMEM((2304, 128), F32)],
    )(tile_density, tile_dest.reshape(1, 64), tile_place.reshape(1, 64))
    arrived = lax.all_to_all(outgoing.reshape(128, 9, 2, 128), ROWS, 0, 0, tiled=True)
    arrived, mix_table, slab_table, phase, final_table, cell_table = (
        lax.optimization_barrier(
            (arrived, mix_table, slab_table, phase, final_table, cell_table)
        )
    )
    sent = pl.pallas_call(
        scatter_body,
        in_specs=[VMEM],
        out_specs=VMEM,
        out_shape=jax.ShapeDtypeStruct((4, 256, 128), BF16),
        compiler_params=GRANT,
        scratch_shapes=[
            pltpu.VMEM((2304, 128), F32),
            pltpu.VMEM((2, 512, 512), BF16),
            pltpu.VMEM((2, 256, 512), BF16),
        ],
    )(in_vmem(arrived.reshape(2304, 128)))

    cells = lax.all_to_all(sent, "cols", 0, 0, tiled=True)
    section_two = pl.pallas_call(
        rows_body,
        in_specs=[VMEM, VMEM, pl.BlockSpec(memory_space=pltpu.HBM), VMEM],
        out_specs=VMEM,
        out_shape=jax.ShapeDtypeStruct((2048, 128), BF16),
        compiler_params=GRANT,
        scratch_shapes=[
            pltpu.VMEM((2048, 128), F32),
            pltpu.VMEM((256, 128), BF16),
            pltpu.SemaphoreType.DMA(()),
        ],
    )(
        in_vmem(cells),
        in_vmem(mix_table),
        pltpu.with_memory_space_constraint(slab_table, pltpu.HBM),
        in_vmem(phase),
    )

    section_two = lax.all_to_all(
        section_two.reshape(512, 2, 2, 128), EVERYWHERE, 0, 0, tiled=True
    )
    return pl.pallas_call(
        final_body,
        in_specs=[VMEM] * 4,
        out_specs=pl.BlockSpec(memory_space=pl.ANY),
        out_shape=jax.ShapeDtypeStruct((256, 2, 512), F32),
        compiler_params=GRANT,
        scratch_shapes=[
            pltpu.VMEM((2048, 128), F32),
            pltpu.VMEM((256, 1024), BF16),
            pltpu.VMEM((512, 512), BF16),
            pltpu.VMEM((256, 2, 512), F32),
            pltpu.SemaphoreType.DMA((4,)),
        ],
    )(
        in_vmem(section_two.reshape(2048, 128)),
        in_vmem(final_table),
        in_vmem(cell_table),
        in_vmem(psf_spectrum),
    )


def solution(mesh):
    rows, cols = mesh.devices.shape
    split = Mesh(mesh.devices.reshape(rows // 2, 2, cols), EVERYWHERE)
    in_specs = (P(EVERYWHERE, None, None), P(EVERYWHERE, None), P(EVERYWHERE), P(ROWS, "cols"))
    return jax.shard_map(
        on_device,
        mesh=split,
        in_specs=in_specs,
        out_specs=P(ROWS, None, "cols"),
        check_vma=False,
    )
```

```python
import math

import jax
import jax.numpy as jnp
from jax import lax
from jax.experimental import pallas as pl
from jax.experimental.pallas import tpu as pltpu
from jax.sharding import Mesh
from jax.sharding import PartitionSpec as P

ROWS = ("chip", "core")
EVERYWHERE = ("chip", "core", "cols")
F32 = jnp.float32
BF16 = jnp.bfloat16


def cosines(index, period):
    return jnp.cos(2.0 * math.pi / period * (index % period).astype(F32))


def lane_group(shape):
    return lax.broadcasted_iota(jnp.int32, shape, 1) // 32


def pack_body(tiles_ref, dest_ref, place_ref, out_ref, flat_ref, packed_ref):
    for tile in range(32):
        start = 64 * tile
        flat_ref[start : start + 64, :64] = tiles_ref[tile].astype(F32)
        flat_ref[start : start + 64, 64:] = tiles_ref[tile + 32].astype(F32)
    place = place_ref[...]
    labels = jnp.concatenate([place // 16 * 128 + dest_ref[...], place % 16], 1).astype(F32)
    group = lax.broadcasted_iota(jnp.int32, (1, 128), 1) // 16
    swapped = jnp.where(
        group % 2 == 0, pltpu.roll(labels, 112, 1), pltpu.roll(labels, 16, 1)
    )
    labels = [jnp.broadcast_to(row, (2, 128)) for row in (labels, swapped)]
    odd = lane_group((16, 128)) % 2 == 1
    for chip in range(64):
        first = flat_ref[pl.ds(chip, 16, stride=64), :]
        second = flat_ref[pl.ds(1024 + chip, 16, stride=64), :]
        values = [
            jnp.where(odd, pltpu.roll(second, 32, 1), first),
            jnp.where(odd, first, pltpu.roll(second, 96, 1)),
        ]
        for core in range(2):
            start = 18 * (2 * chip + core)
            packed_ref[start : start + 16] = values[core]
            packed_ref[start + 16 : start + 18] = labels[core]
    out_ref[...] = packed_ref[...].astype(BF16)


def scatter_body(tiles_ref, out_ref, flat_ref, spread_ref, hot_ref):
    flat_ref[...] = tiles_ref[...].astype(F32)
    labels = flat_ref[pl.ds(16, 128, stride=18), :]
    named = jnp.transpose(labels)
    group = lane_group((128, 128))
    lane = group.astype(F32)
    slab = lax.broadcasted_iota(jnp.int32, (256, 128), 0).astype(F32)
    total = None
    for step in range(16):
        slot = step % 2
        values = flat_ref[pl.ds(step, 128, stride=18), :]
        rolls = [values] + [pltpu.roll(values, 32 * j, 1) for j in range(1, 4)]
        for g in range(4):
            copies = rolls[(-g) % 4]
            for h in range(1, 4):
                copies = jnp.where(group == h, rolls[(h - g) % 4], copies)
            copies = copies.astype(BF16)
            tile = 16 * g + step
            place = jnp.broadcast_to(labels[:, 64 + tile : 65 + tile], (128, 128)) - lane
            place = place.astype(BF16)
            for m in range(4):
                spread_ref[slot, 128 * g : 128 * g + 128, 128 * m : 128 * m + 128] = jnp.where(
                    place == jnp.array(4.0 * m, BF16), copies, jnp.zeros_like(copies)
                )
            hot = jnp.broadcast_to(named[tile : tile + 1, :], (256, 128)) == slab
            hot_ref[slot, :, 128 * g : 128 * g + 128] = jnp.where(hot, 1.0, 0.0).astype(BF16)
        part = jnp.dot(hot_ref[slot], spread_ref[slot], preferred_element_type=F32)
        total = part if total is None else total + part
    total = total.astype(BF16)
    lane = lax.broadcasted_iota(jnp.int32, (512, 128), 1)
    source = lane // 8 * 32 + lane % 8
    given = lax.broadcasted_iota(jnp.int32, (512, 128), 0)
    for octet in range(4):
        order = jnp.where(given == source + 8 * octet, 1.0, 0.0).astype(BF16)
        out_ref[octet] = jnp.dot(total, order, preferred_element_type=F32).astype(BF16)


def lane_sign(shape):
    lane = lax.broadcasted_iota(jnp.int32, shape, 1)
    return jnp.where(lane < 64, 1.0, -1.0)


def rows_body(cells_ref, tables_ref, phase_hbm, out_ref, flat_ref, phase_ref, sem):
    fetch = pltpu.make_async_copy(phase_hbm, phase_ref, sem)
    fetch.start()
    sign = lane_sign((128, 128))
    left = lax.broadcasted_iota(jnp.int32, (256, 128), 1) < 64
    for low in range(2):
        pairs = []
        for e in (0, 2):
            first, second = cells_ref[e].astype(F32), cells_ref[e + 1].astype(F32)
            if low == 0:
                second = pltpu.roll(second, 64, 1)
            else:
                first = pltpu.roll(first, 64, 1)
            pairs.append(jnp.where(left, first, second).astype(BF16))
        spectrum = jnp.dot(
            jnp.concatenate(pairs, 1), tables_ref[:, :512], preferred_element_type=F32
        ).astype(BF16)
        for half in range(2):
            r = 2 * half + low
            values = spectrum[128 * half : 128 * half + 128]
            both = jnp.dot(tables_ref[:, 512:], values, preferred_element_type=F32)
            first, second = both[:128], both[128:]
            if r == 0:
                fetch.wait()
            cosine, sine = phase_ref[:, r : r + 1], phase_ref[:, 4 + r : 5 + r]
            straight = first * cosine - second * sine
            crossed = second * cosine + first * sine
            for k in range(4):
                lanes = slice(128 * k, 128 * k + 128)
                flat_ref[pl.ds(4 * k + r, 128, stride=16), :] = straight[
                    :, lanes
                ] + sign * pltpu.roll(crossed[:, lanes], 64, 1)
    out_ref[...] = flat_ref[...].astype(BF16)


def final_body(
    rows_ref,
    table_ref,
    cell_table_ref,
    psf_ref,
    out_ref,
    flat_ref,
    values_ref,
    stacked_ref,
    result_ref,
    sems,
):
    flat_ref[...] = rows_ref[...].astype(F32)
    for h in range(8):
        for r in range(4):
            values_ref[64 * r : 64 * r + 64, 128 * h : 128 * h + 128] = flat_ref[
                pl.ds(4 * h + r, 64, stride=32), :
            ].astype(BF16)
    spectrum = jnp.dot(values_ref[...], cell_table_ref[...], preferred_element_type=F32)
    stacked_ref[:256] = spectrum[:, :512].astype(BF16)
    stacked_ref[256:] = spectrum[:, 512:].astype(BF16)
    copies = []
    for part in range(4):
        window = pl.ds(64 * part, 64)
        result = jnp.dot(
            table_ref[128 * part : 128 * part + 128, :],
            stacked_ref[...],
            preferred_element_type=F32,
        )
        psf = psf_ref[window, :].astype(F32)
        result_ref[window, 0, :] = result[:64] * psf
        result_ref[window, 1, :] = result[64:] * psf
        copy = pltpu.make_async_copy(result_ref.at[window], out_ref.at[window], sems.at[part])
        copy.start()
        copies.append(copy)
    for copy in copies:
        copy.wait()


VMEM = pl.BlockSpec(memory_space=pltpu.VMEM)
GRANT = pltpu.CompilerParams(vmem_limit_bytes=16 * 2**20)


def in_vmem(x):
    return pltpu.with_memory_space_constraint(x, pltpu.VMEM)


def on_device(tile_density, tile_dest, tile_place, psf_spectrum):
    chip = lax.axis_index("chip")
    core = lax.axis_index("core")
    me_col = lax.axis_index("cols")
    iota = lambda n: jnp.arange(n, dtype=jnp.int32)

    member = 4 * core + me_col

    given, out = iota(256)[:, None], iota(512)[None, :]
    column = given // 8 * 64 + 8 * member + given % 8
    frequency = out // 128 + 4 * (out % 64 // 8)
    mix_table = cosines(column * frequency + 512 * (out % 128 // 64), 2048)
    mix_table = jnp.where(
        given % 8 == out % 8, mix_table * (1.0 / math.sqrt(2048)), 0.0
    ).astype(BF16)

    given, out = iota(128)[None, :], iota(256)[:, None]
    slab_table = cosines(given * (out % 128) + 96 * (out // 128), 128).astype(BF16)
    tables = jnp.concatenate([mix_table, slab_table], 1)
    part = iota(8)[None, :]
    phase = cosines(
        (64 * (part % 4) + chip) * iota(128)[:, None] + 24576 * (part // 4), 32768
    )

    given, out = iota(512)[None, :], iota(512)[:, None]
    frequency = out // 128 * 64 + out % 64
    turn = 64 * (out % 128 // 64) - 64 * (given // 256) + 256
    final_table = cosines(given % 256 * frequency + turn, 256)
    final_table = (final_table * (1.0 / math.sqrt(32768))).astype(BF16)

    given, out = iota(128)[:, None], iota(128)[None, :]
    turn = 16 * (out // 64 - given % 16 // 8) + 64
    cell_table = cosines((given // 16 * 8 + given % 8) * (out % 64) + turn, 64).astype(BF16)
    given, out = iota(1024)[:, None], iota(1024)[None, :]
    from_rows = given // 64 * 8 + given % 8 == iota(128)[None, :]
    to_columns = iota(128)[:, None] == out // 8
    cell_table = jnp.dot(from_rows.astype(BF16), cell_table)
    cell_table = jnp.dot(cell_table, to_columns.astype(BF16))
    cell_table = jnp.where(given % 64 // 8 == out % 8, cell_table, jnp.zeros_like(cell_table))

    outgoing = pl.pallas_call(
        pack_body,
        in_specs=[VMEM] * 3,
        out_specs=VMEM,
        out_shape=jax.ShapeDtypeStruct((2304, 128), BF16),
        scratch_shapes=[pltpu.VMEM((2048, 128), F32), pltpu.VMEM((2304, 128), F32)],
    )(tile_density, tile_dest.reshape(1, 64), tile_place.reshape(1, 64))
    arrived = lax.all_to_all(outgoing.reshape(128, 9, 2, 128), ROWS, 0, 0, tiled=True)
    arrived, tables, phase, final_table, cell_table = lax.optimization_barrier(
        (arrived, tables, phase, final_table, cell_table)
    )
    sent = pl.pallas_call(
        scatter_body,
        in_specs=[VMEM],
        out_specs=VMEM,
        out_shape=jax.ShapeDtypeStruct((4, 256, 128), BF16),
        compiler_params=GRANT,
        scratch_shapes=[
            pltpu.VMEM((2304, 128), F32),
            pltpu.VMEM((2, 512, 512), BF16),
            pltpu.VMEM((2, 256, 512), BF16),
        ],
    )(in_vmem(arrived.reshape(2304, 128)))

    cells = lax.all_to_all(sent, "cols", 0, 0, tiled=True)
    section_two = pl.pallas_call(
        rows_body,
        in_specs=[VMEM, VMEM, pl.BlockSpec(memory_space=pltpu.HBM)],
        out_specs=VMEM,
        out_shape=jax.ShapeDtypeStruct((2048, 128), BF16),
        compiler_params=GRANT,
        scratch_shapes=[
            pltpu.VMEM((2048, 128), F32),
            pltpu.VMEM((128, 8), F32),
            pltpu.SemaphoreType.DMA(()),
        ],
    )(
        in_vmem(cells),
        in_vmem(tables),
        pltpu.with_memory_space_constraint(phase, pltpu.HBM),
    )

    section_two = lax.all_to_all(
        section_two.reshape(512, 2, 2, 128), EVERYWHERE, 0, 0, tiled=True
    )
    return pl.pallas_call(
        final_body,
        in_specs=[VMEM] * 4,
        out_specs=pl.BlockSpec(memory_space=pl.ANY),
        out_shape=jax.ShapeDtypeStruct((256, 2, 512), F32),
        compiler_params=GRANT,
        scratch_shapes=[
            pltpu.VMEM((2048, 128), F32),
            pltpu.VMEM((256, 1024), BF16),
            pltpu.VMEM((512, 512), BF16),
            pltpu.VMEM((256, 2, 512), F32),
            pltpu.SemaphoreType.DMA((4,)),
        ],
    )(
        in_vmem(section_two.reshape(2048, 128)),
        in_vmem(final_table),
        in_vmem(cell_table),
        in_vmem(psf_spectrum),
    )


def solution(mesh):
    rows, cols = mesh.devices.shape
    split = Mesh(mesh.devices.reshape(rows // 2, 2, cols), EVERYWHERE)
    in_specs = (P(EVERYWHERE, None, None), P(EVERYWHERE, None), P(EVERYWHERE), P(ROWS, "cols"))
    return jax.shard_map(
        on_device,
        mesh=split,
        in_specs=in_specs,
        out_specs=P(ROWS, None, "cols"),
        check_vma=False,
    )
```
